256 devices in a mesh: panel: 32 (over z, y_lo, core), rep: 8 (over x, y_hi).
Axes of the slice: x: 4, y: 4 (y_hi: 2, y_lo: 2; y = y_hi * 2 + y_lo), z: 8, core: 2. Of those that a mesh axis runs over, the one named last changes fastest.
Arguments:
- x_src: bfloat16 [4096, 128], P('panel'), may hold values from -6 to 6
- x_dst: bfloat16 [131072, 128], P(('panel', 'rep')), may hold values from -6 to 6
- weight: bfloat16 [128, 512], replicated, may hold values from -0.5 to 0.5
- att_src: float32 [8, 64], replicated, may hold values from -0.75 to 0.75
- att_dst: float32 [8, 64], replicated, may hold values from -0.75 to 0.75
- grad_out: bfloat16 [131072, 512], P(('panel', 'rep')), may hold values from -6 to 6
- block_rows: int32 [4096], P(('panel', 'rep')), may hold values from 0 to 3, as said below
- block_cols: int32 [4096], P(('panel', 'rep')), may hold values from 0 to 31
- block_masks: int32 [4096, 128, 128], P(('panel', 'rep')), may hold values from 0 to 1, as said below
- block_counts: int32 [256], P(('panel', 'rep')), may hold values from 2 to 16, as said below
Outputs:
- grad_src: float32 [4096, 128], P('panel')
- grad_dst: float32 [131072, 128], P(('panel', 'rep'))
- grad_weight: float32 [128, 512], replicated
- grad_att_src: float32 [8, 64], replicated
- grad_att_dst: float32 [8, 64], replicated
The draws below stay inside these ranges and needn't reach their ends.
Inputs may be any that keep to these rules, and one draw needn't show every extreme that they name: `block_counts`: live block slots of one device; at least one device has exactly 16. The pairs of block_rows and block_cols within one device's 16 slots are distinct. `block_masks`: slots at or after a device's count of live blocks hold only zeros.
All inputs are finite; a program needn't handle non-finite values.
Results may differ from the reference program's by a relative error of at most 0.012.
The reference program's roundings to bfloat16 on the way (of `proj_src` and `proj_dst`) count: a program that leaves them out, or rounds other values in their place, can miss the bound.
Values may be sent and summed in bfloat16 or wider, within the bound.
No kernel may reach another device: no remote copies, remote signals or barrier semaphores. Data moves between devices by JAX's collectives and lax.ppermute only.
A program may use at most 128 MiB of HBM per device.

```python
import jax
import jax.numpy as jnp
from jax import lax

HEADS = 8
HEAD_DIM = 64
IN = 128
WIDTH = 512
BLK = 128
DST_DEV = 512
NB_DEV = 16
NSRC = 4096
NDST = 131072
N_PANEL = 32
N_REP = 8


def block_layout(key):
    device_count = N_PANEL * N_REP
    dest_blocks = DST_DEV // BLK
    source_blocks = NSRC // BLK
    keys_all = jax.random.split(jax.random.fold_in(key, 17), 5)
    halvings = jax.random.randint(keys_all[0], (device_count,), 0, 4)
    fullest = jax.random.randint(keys_all[1], (), 0, device_count)
    halvings = jnp.where(jnp.arange(device_count) == fullest, 0, halvings).astype(jnp.int32)
    live_counts = jnp.right_shift(jnp.full((device_count,), NB_DEV, jnp.int32), halvings)
    pair_keys = jax.random.split(keys_all[2], device_count)

    def pick_pairs(one_key):
        return jax.random.permutation(one_key, dest_blocks * source_blocks)[:NB_DEV]
    pair_codes = jax.vmap(pick_pairs)(pair_keys).astype(jnp.int32)
    rows_drawn = (pair_codes // source_blocks).reshape(-1).astype(jnp.int32)
    cols_drawn = (pair_codes % source_blocks).reshape(-1).astype(jnp.int32)
    density = jax.random.randint(keys_all[3], (device_count, NB_DEV, 1, 1), 64, 512)
    edge_bits = jax.random.randint(keys_all[4], (device_count, NB_DEV, BLK, BLK), 0, 1024) < density
    live_slots = (jnp.arange(NB_DEV)[None, :] < live_counts[:, None])[:, :, None, None]
    masks_drawn = jnp.where(edge_bits & live_slots, 1, 0).astype(jnp.int32).reshape(device_count * NB_DEV, BLK, BLK)
    return (live_counts, rows_drawn, cols_drawn, masks_drawn)


def draw_block_counts(key, part):
    return block_layout(key)[0]


def draw_block_rows(key, part):
    return block_layout(key)[1]


def draw_block_cols(key, part):
    return block_layout(key)[2]


def draw_block_masks(key, part):
    return block_layout(key)[3]


def level_of(key, dims, pieces, least, high):
    level, own = 1.0, jax.random.fold_in(key, 6)
    for dim, parts in pieces:
        draws = jnp.exp(jax.random.uniform(jax.random.fold_in(own, dim), (parts,), jnp.float32, least / len(pieces), high / len(pieces)))
        level = level * jnp.repeat(draws, dims[dim] // parts).reshape([-1 if axis == dim else 1 for axis in range(len(dims))])
    return level


def scatter_about(rng, extent, width, limit, shards=(), kind=jnp.bfloat16):
    array = width * jax.random.normal(rng, extent, jnp.float32)
    if shards:
        array = array * level_of(rng, extent, shards, -0.22, 0.18)
    return jnp.clip(array, -limit, limit).astype(kind)


def setup_inputs(seed: int = 0) -> dict:
    arg_keys = jax.random.split(jax.random.key(seed), 11)
    return {
        "x_src": scatter_about(arg_keys[0], (NSRC, IN), 1.0, 6.0, ((0, 32),)),
        "x_dst": scatter_about(arg_keys[1], (NDST, IN), 1.0, 6.0, ((0, 256),)),
        "weight": scatter_about(arg_keys[2], (IN, WIDTH), IN ** -0.5, 0.5),
        "att_src": scatter_about(arg_keys[3], (HEADS, HEAD_DIM), HEAD_DIM ** -0.5, 0.75, (), jnp.float32),
        "att_dst": scatter_about(arg_keys[4], (HEADS, HEAD_DIM), HEAD_DIM ** -0.5, 0.75, (), jnp.float32),
        "grad_out": scatter_about(arg_keys[5], (NDST, WIDTH), 1.0, 6.0, ((0, 256),)),
        "block_rows": draw_block_rows(jax.random.fold_in(arg_keys[10], 71), 0),
        "block_cols": draw_block_cols(jax.random.fold_in(arg_keys[10], 71), 0),
        "block_masks": draw_block_masks(jax.random.fold_in(arg_keys[10], 71), 0),
        "block_counts": draw_block_counts(jax.random.fold_in(arg_keys[10], 71), 0),
    }


HIGHEST_PRECISION = lax.Precision.HIGHEST


def smooth_leaky(values):
    return 0.2 * values + 0.8 * jax.nn.softplus(values)


def smooth_slope(values):
    return 0.2 + 0.8 * jax.nn.sigmoid(values)


def to_bfloat(values):
    return lax.optimization_barrier(values.astype(jnp.bfloat16)).astype(jnp.float32)


def add_slice(target, update, start, axis):
    current = lax.dynamic_slice_in_dim(target, start, update.shape[axis], axis)
    return lax.dynamic_update_slice_in_dim(target, current + update, start, axis)


def reference(x_src, x_dst, weight, att_src, att_dst, grad_out, block_rows, block_cols, block_masks, block_counts):
    device_count = N_PANEL * N_REP
    proj_src = jnp.dot(x_src, weight, preferred_element_type=jnp.float32).astype(jnp.bfloat16)
    source_feats = proj_src.astype(jnp.float32).reshape(NSRC, HEADS, HEAD_DIM)
    score_src = jnp.einsum("jhk,hk->hj", source_feats, att_src, precision=HIGHEST_PRECISION)
    proj_dst = jnp.dot(x_dst, weight, preferred_element_type=jnp.float32).astype(jnp.bfloat16)
    dest_feats = proj_dst.astype(jnp.float32).reshape(NDST, HEADS, HEAD_DIM)
    score_dst = jnp.einsum("ihk,hk->hi", dest_feats, att_dst, precision=HIGHEST_PRECISION)
    score_self = jnp.einsum("ihk,hk->hi", dest_feats, att_src, precision=HIGHEST_PRECISION)
    cotangent = grad_out.astype(jnp.float32).reshape(NDST, HEADS, HEAD_DIM)
    rows_all = block_rows.reshape(device_count, NB_DEV)
    cols_all = block_cols.reshape(device_count, NB_DEV)
    masks_all = block_masks.reshape(device_count, NB_DEV, BLK, BLK)

    def device_step(carried, device):
        grad_source, grad_score_src = carried
        row_start = device * DST_DEV
        feats = lax.dynamic_slice_in_dim(dest_feats, row_start, DST_DEV, 0)
        cotan = lax.dynamic_slice_in_dim(cotangent, row_start, DST_DEV, 0)
        score_d = lax.dynamic_slice_in_dim(score_dst, row_start, DST_DEV, 1)
        score_own = lax.dynamic_slice_in_dim(score_self, row_start, DST_DEV, 1)
        dest_index = rows_all[device]
        source_index = cols_all[device]
        masks = masks_all[device]
        live_count = block_counts[device]

        def block_scores(block_index):
            dest_block = dest_index[block_index] * BLK
            source_block = source_index[block_index] * BLK
            pre_score = (lax.dynamic_slice_in_dim(score_d, dest_block, BLK, 1)[:, :, None]
                         + lax.dynamic_slice_in_dim(score_src, source_block, BLK, 1)[:, None, :])
            edge_weight = jnp.exp(smooth_leaky(pre_score)) * masks[block_index].astype(jnp.float32)[None]
            source_rows = lax.dynamic_slice_in_dim(source_feats, source_block, BLK, 0)
            return dest_block, source_block, pre_score, edge_weight, source_rows

        def forward_block(block_index, carried_fwd):
            denominator, numerator = carried_fwd
            dest_block, source_block, pre_score, edge_weight, source_rows = block_scores(block_index)
            part_num = jnp.einsum("hij,jhk->ihk", to_bfloat(edge_weight), source_rows, precision=HIGHEST_PRECISION)
            denominator = add_slice(denominator, edge_weight.sum(axis=2), dest_block, 1)
            numerator = add_slice(numerator, part_num, dest_block, 0)
            return denominator, numerator

        zero_start = jnp.int32(0)
        denominator, numerator = lax.fori_loop(zero_start, live_count, forward_block,
                                               (jnp.zeros((HEADS, DST_DEV), jnp.float32),
                                                jnp.zeros((DST_DEV, HEADS, HEAD_DIM), jnp.float32)))
        pre_self = score_d + score_own
        self_weight = jnp.exp(smooth_leaky(pre_self))
        denominator = denominator + self_weight
        numerator = numerator + self_weight.T[:, :, None] * feats
        attended = numerator / denominator.T[:, :, None]
        centred = jnp.sum(cotan * attended, axis=2).T

        def backward_block(block_index, carried_bwd):
            grad_source, grad_score_src, grad_score_dst = carried_bwd
            dest_block, source_block, pre_score, edge_weight, source_rows = block_scores(block_index)
            attention = edge_weight / lax.dynamic_slice_in_dim(denominator, dest_block, BLK, 1)[:, :, None]
            cotan_rows = lax.dynamic_slice_in_dim(cotan, dest_block, BLK, 0)
            pair_grad = jnp.einsum("ihk,jhk->hij", cotan_rows, source_rows, precision=HIGHEST_PRECISION)
            centred_rows = lax.dynamic_slice_in_dim(centred, dest_block, BLK, 1)
            score_grad = attention * (pair_grad - centred_rows[:, :, None]) * smooth_slope(pre_score)
            feat_grad = jnp.einsum("hij,ihk->jhk", to_bfloat(attention), cotan_rows, precision=HIGHEST_PRECISION)
            grad_source = add_slice(grad_source, feat_grad, source_block, 0)
            grad_score_src = add_slice(grad_score_src, score_grad.sum(axis=1), source_block, 1)
            grad_score_dst = add_slice(grad_score_dst, score_grad.sum(axis=2), dest_block, 1)
            return grad_source, grad_score_src, grad_score_dst

        grad_source, grad_score_src, grad_score_dst = lax.fori_loop(
            zero_start, live_count, backward_block,
            (grad_source, grad_score_src, jnp.zeros((HEADS, DST_DEV), jnp.float32)))
        self_attention = self_weight / denominator
        self_pair = jnp.sum(cotan * feats, axis=2).T
        self_grad = self_attention * (self_pair - centred) * smooth_slope(pre_self)
        grad_score_dst = grad_score_dst + self_grad
        grad_dest = (self_attention.T[:, :, None] * cotan + self_grad.T[:, :, None] * att_src[None]
                     + grad_score_dst.T[:, :, None] * att_dst[None])
        att_self = jnp.einsum("hi,ihk->hk", self_grad, feats, precision=HIGHEST_PRECISION)
        att_dest = jnp.einsum("hi,ihk->hk", grad_score_dst, feats, precision=HIGHEST_PRECISION)
        return (grad_source, grad_score_src), (grad_dest, att_self, att_dest)

    initial = (jnp.zeros((NSRC, HEADS, HEAD_DIM), jnp.float32), jnp.zeros((HEADS, NSRC), jnp.float32))
    (grad_source, grad_score_src), (grad_dest, att_self, att_dest) = lax.scan(
        device_step, initial, jnp.arange(device_count, dtype=jnp.int32))
    grad_source = grad_source + grad_score_src.T[:, :, None] * att_src[None]
    grad_att_src = jnp.einsum("hj,jhk->hk", grad_score_src, source_feats, precision=HIGHEST_PRECISION) + att_self.sum(axis=0)
    grad_att_dst = att_dest.sum(axis=0)
    source_flat = grad_source.reshape(NSRC, WIDTH)
    dest_flat = grad_dest.reshape(NDST, WIDTH)
    weight_t = weight.astype(jnp.float32).T
    grad_src = jnp.dot(source_flat, weight_t, precision=HIGHEST_PRECISION)
    grad_dst = jnp.dot(dest_flat, weight_t, precision=HIGHEST_PRECISION)
    grad_weight = (jnp.dot(x_src.astype(jnp.float32).T, source_flat, precision=HIGHEST_PRECISION)
                   + jnp.dot(x_dst.astype(jnp.float32).T, dest_flat, precision=HIGHEST_PRECISION))
    return grad_src, grad_dst, grad_weight, grad_att_src, grad_att_dst
```

```python
import jax
import jax.numpy as jnp
from jax import lax
from jax.experimental import pallas as pl
from jax.experimental.pallas import tpu as pltpu
from jax.sharding import PartitionSpec as P

HEADS, HEAD_DIM, IN, WIDTH, BLK = 8, 64, 128, 512, 128
LOG2E = 1.4426950408889634
LANES = 128
F32, BF16 = jnp.float32, jnp.bfloat16
VMEM_BYTES = 40 << 20
SPREAD = 32

NN = (((1,), (0,)), ((), ()))
NT = (((1,), (1,)), ((), ()))
TN = (((0,), (0,)), ((), ()))


def mm(a, b, dims=NN):
    return lax.dot_general(a, b, dims, preferred_element_type=F32)


def split2(values):
    hi = values.astype(BF16)
    return hi, (values - hi.astype(F32)).astype(BF16)


def split3(values):
    hi = values.astype(BF16)
    rest = values - hi.astype(F32)
    mid = rest.astype(BF16)
    return hi, mid, (rest - mid.astype(F32)).astype(BF16)


def head_rows(att_flat):
    head = lax.broadcasted_iota(jnp.int32, (HEADS, WIDTH), 0)
    lane = lax.broadcasted_iota(jnp.int32, (HEADS, WIDTH), 1) // HEAD_DIM
    return jnp.where(head == lane, jnp.broadcast_to(att_flat, (HEADS, WIDTH)), 0.0)


def per_head(rows):
    width = rows.shape[1]
    return jnp.concatenate(
        [jnp.broadcast_to(rows[h : h + 1], (HEAD_DIM, width)) for h in range(HEADS)], axis=0
    )


def head_sums(values):
    return jnp.concatenate(
        [
            jnp.sum(values[h * HEAD_DIM : (h + 1) * HEAD_DIM], axis=0, keepdims=True)
            for h in range(HEADS)
        ],
        axis=0,
    )


def weight_and_slope(pre2):
    log = jnp.log2(1.0 + jnp.exp2(pre2))
    return jnp.exp2(0.2 * pre2 + 0.8 * log), 1.0 - 0.8 * jnp.exp2(-log)


def prepare(
    x_dst_ref, weight_ref, att_src_ref, att_dst_ref, grad_ref, mask_ref,
    proj_ref, grad_t_ref, mask_t_ref, spread_ref, self_ref, slope_ref, pair_ref,
):
    weight_t = weight_ref[...].astype(F32).T.astype(BF16)
    proj = mm(weight_t, x_dst_ref[...], NT).astype(BF16)
    proj_ref[...] = proj
    grad_t = grad_ref[...].astype(F32).T
    grad_t_ref[...] = grad_t.astype(BF16)
    parts = split3(head_rows(att_dst_ref[...])) + split3(head_rows(att_src_ref[...]))
    scores = mm(jnp.concatenate(parts, axis=0), proj)
    score_d = (scores[0:8] + scores[8:16]) + scores[16:24]
    score_own = (scores[24:32] + scores[32:40]) + scores[40:48]
    kind = lax.broadcasted_iota(jnp.int32, (SPREAD - HEADS, HEADS * BLK), 0)
    lane_head = lax.broadcasted_iota(jnp.int32, (SPREAD - HEADS, HEADS * BLK), 1) // BLK
    ones = jnp.where(kind % HEADS == lane_head, 1.0, 0.0)
    for r in range(spread_ref.shape[0]):
        line = jnp.concatenate(
            [score_d[h : h + 1, r * BLK : (r + 1) * BLK] for h in range(HEADS)], axis=1
        ) * LOG2E
        parts = [p.astype(F32) for p in split3(line)]
        rest = jnp.zeros((HEADS - len(parts), HEADS * BLK), F32)
        spread_ref[r] = jnp.concatenate([ones, *parts, rest], axis=0).astype(BF16)
    weight_self, slope_self = weight_and_slope((score_d + score_own) * LOG2E)
    self_ref[...] = weight_self
    slope_ref[...] = slope_self
    pair_ref[...] = head_sums(grad_t * proj.astype(F32))

    def turn(b, carry):
        mask_t_ref[b] = mask_ref[b].astype(F32).T
        return carry

    lax.fori_loop(0, mask_ref.shape[0], turn, 0)


def edges(
    rows_ref, cols_ref, place_ref,
    x_own_ref, x_other_ref, x_dst_ref, weight_ref, att_src_ref, att_src_col_ref, att_dst_col_ref,
    proj_ref, grad_t_ref, mask_t_ref, spread_ref, self_ref, slope_ref, pair_ref,
    grad_dst_ref, keep_ref, send_ref,
    proj_src, tiles, acc, scaled, scaled_c, own, grad_src_ref, grad_weight_ref, rows_out, score_cols, att_wide, x_all,
):
    slots = mask_t_ref.shape[0]
    dest_blocks = acc.shape[0]
    ext = acc.shape[2]
    weight = weight_ref[...]
    weight_t = weight.astype(F32).T.astype(BF16)
    att_rows = jnp.concatenate(split3(head_rows(att_src_ref[...])), axis=0)
    acc[...] = jnp.zeros(acc.shape, F32)
    grad_src_ref[...] = jnp.zeros(grad_src_ref.shape, grad_src_ref.dtype)
    ones = jnp.ones((ext - HEAD_DIM, BLK), BF16)

    att_wide[...] = jnp.broadcast_to(att_src_col_ref[...], att_wide.shape)

    core = place_ref[0] % 2
    half = x_own_ref.shape[0]
    x_all[0:half] = x_own_ref[...]
    x_all[half : 2 * half] = x_other_ref[...]

    def block(b):
        return pl.ds(pl.multiple_of(cols_ref[b] * BLK, BLK), BLK)

    def sources(b):
        col = cols_ref[b]
        place = (col % 2 + core) % 2 * half + col // 2 * BLK
        return x_all[pl.ds(pl.multiple_of(place, BLK), BLK), :]

    def project(step, carry):
        b = 2 * step
        pair = jnp.concatenate([sources(b), sources(b + 1)], axis=0)
        proj = mm(weight_t, pair, NT).astype(BF16)
        scores = mm(att_rows, proj)
        parts = split3(((scores[0:8] + scores[8:16]) + scores[16:24]) * LOG2E)
        tail = lax.broadcasted_iota(jnp.int32, (HEADS, 2 * BLK), 0)
        tail = jnp.where(tail < len(parts), 1.0, 0.0)
        cols = jnp.concatenate([*(p.astype(F32) for p in parts), tail], axis=0).T.astype(BF16)
        for k in range(2):
            proj_src[b + k] = proj[:, k * BLK : (k + 1) * BLK]
            score_cols[b + k] = cols[k * BLK : (k + 1) * BLK]
        return carry

    lax.fori_loop(0, slots // 2, project, 0, unroll=1)

    def forward(b, carry):
        row = rows_ref[b]
        proj = proj_src[b]
        cols = score_cols[b]
        mask = mask_t_ref[b]
        colsf = (cols[:,0:8].astype(F32)+cols[:,8:16].astype(F32))+cols[:,16:24].astype(F32)
        srow = (spread_ref[row,24:32].astype(F32)).sum(axis=0,keepdims=True)
        for h in range(HEADS):
            lanes = slice(h * BLK, (h + 1) * BLK)
            weight_e, slope = weight_and_slope(jnp.broadcast_to(colsf[:, h:h+1],(BLK,BLK)) + srow[:, lanes])
            weight_e = weight_e * mask
            pair = jnp.concatenate(
                [weight_e.astype(BF16), (weight_e * slope).astype(BF16)], axis=1
            )
            tiles[b, h] = pair
            left = jnp.concatenate([proj[h * HEAD_DIM : (h + 1) * HEAD_DIM], ones], axis=0)
            acc[row, h] += mm(left, pair)
        return carry

    lax.fori_loop(0, slots, forward, 0, unroll=2)

    self_att_rows, self_grad_rows, grad_d_rows = [], [], []
    for r in range(dest_blocks):
        lanes = slice(r * BLK, (r + 1) * BLK)
        self_w = self_ref[:, lanes]
        selfs, grads, dsts = [], [], []
        for h in range(HEADS):
            feats = slice(h * HEAD_DIM, (h + 1) * HEAD_DIM)
            sums = acc[r, h]
            w_self = self_w[h : h + 1]
            inv = 1.0 / (sums[HEAD_DIM : HEAD_DIM + 1, :BLK] + w_self)
            numer = sums[:HEAD_DIM, :BLK] + w_self * proj_ref[feats, lanes].astype(F32)
            grad = grad_t_ref[feats, lanes].astype(F32)
            part = (grad * inv).astype(BF16)
            part_wide = part.astype(F32)
            centred = jnp.sum(grad * numer, axis=0, keepdims=True) * inv
            centred_part = jnp.sum(part_wide * numer, axis=0, keepdims=True) * inv
            grad_d = (
                jnp.sum(part_wide * sums[:HEAD_DIM, BLK:], axis=0, keepdims=True)
                - centred_part * sums[HEAD_DIM : HEAD_DIM + 1, BLK:]
            )
            att_self = w_self * inv
            grad_self = (
                att_self * (pair_ref[h : h + 1, lanes] - centred) * slope_ref[h : h + 1, lanes]
            )
            scaled[r, h, 0:HEAD_DIM] = part
            c_hi, c_lo = split2(centred_part)
            scaled_c[r, h, 0:1] = c_hi.astype(F32)
            scaled_c[r, h, 1:2] = c_lo.astype(F32)
            selfs.append(att_self)
            grads.append(grad_self)
            dsts.append(grad_d + grad_self)
        self_att_rows.append(jnp.concatenate(selfs, axis=0))
        self_grad_rows.append(jnp.concatenate(grads, axis=0))
        grad_d_rows.append(jnp.concatenate(dsts, axis=0))
    for r in range(dest_blocks):
        for h in range(HEADS):
            scaled[r, h, HEAD_DIM:ext] = jnp.concatenate(
                [scaled_c[r, h, 0:2], jnp.zeros((ext - HEAD_DIM - 2, BLK), F32)], axis=0
            ).astype(BF16)

    att_src_wide = att_wide[...]
    att_dst_wide = jnp.broadcast_to(att_dst_col_ref[...], att_wide.shape)
    grad_weight = jnp.zeros((WIDTH, IN), F32)
    att_sums = jnp.zeros((WIDTH, 32), F32)
    for r in range(dest_blocks):
        lanes = slice(r * BLK, (r + 1) * BLK)
        grad_proj = (
            per_head(self_att_rows[r]) * grad_t_ref[:, lanes].astype(F32)
            + per_head(self_grad_rows[r]) * att_src_wide
            + per_head(grad_d_rows[r]) * att_dst_wide
        ).astype(BF16)
        grad_dst_ref[lanes, :] = mm(weight, grad_proj).T
        grad_weight = grad_weight + mm(grad_proj, x_dst_ref[lanes, :])
        both = jnp.concatenate(split2(self_grad_rows[r]) + split2(grad_d_rows[r]), axis=0)
        att_sums = att_sums + mm(proj_ref[:, lanes], both, NT)
    grad_weight_ref[...] = grad_weight
    own[...] = att_sums

    def back(b):
        row = rows_ref[b]
        proj = proj_src[b]
        feats, grads = [], []
        for h in range(HEADS):
            pair = tiles[b, h]
            stack = jnp.concatenate([pair[:, :BLK], pair[:, BLK:]], axis=0)
            out = mm(scaled[row, h], stack, NT)
            feats.append(out[:HEAD_DIM, :BLK])
            proj_h = proj[h * HEAD_DIM : (h + 1) * HEAD_DIM].astype(F32)
            grads.append(
                jnp.sum(proj_h * out[:HEAD_DIM, BLK:], axis=0, keepdims=True)
                - (out[HEAD_DIM : HEAD_DIM + 1, BLK:] + out[HEAD_DIM + 1 : HEAD_DIM + 2, BLK:])
            )
        grad_s = jnp.concatenate(grads, axis=0)
        grad_proj = jnp.concatenate(feats, axis=0) + per_head(grad_s) * att_wide[...]
        return proj, grad_s, grad_proj.astype(BF16)

    def backward(step, carry):
        b = 2 * step
        projs, grads, parts = zip(back(b), back(b + 1))
        grad_proj = jnp.concatenate(parts, axis=1)
        into = mm(weight, grad_proj)
        x_pair = jnp.concatenate([sources(b), sources(b + 1)], axis=0)
        grad_weight_ref[...] += mm(grad_proj, x_pair)
        grad_s = jnp.concatenate(split2(jnp.concatenate(grads, axis=1)), axis=0)
        own[:, 0:16] += mm(jnp.concatenate(projs, axis=1), grad_s, NT)
        for k in range(2):
            grad_src_ref[block(b + k), :] += into[:, k * BLK : (k + 1) * BLK].T
        return carry

    lax.fori_loop(0, slots // 2, backward, 0, unroll=2)

    sums = own[...]
    head = lax.broadcasted_iota(jnp.int32, (WIDTH, HEADS), 1)
    feat = lax.broadcasted_iota(jnp.int32, (WIDTH, HEADS), 0) // HEAD_DIM
    pick = head == feat
    src = jnp.where(pick, sums[:, 0:8] + sums[:, 8:16], 0.0)
    dst = jnp.where(pick, sums[:, 16:24] + sums[:, 24:32], 0.0)
    att_rows8 = [
        jnp.sum(part[f : f + LANES].T, axis=0, keepdims=True)
        for part in (src, dst)
        for f in range(0, WIDTH, LANES)
    ]
    att8 = jnp.concatenate(att_rows8, axis=0)
    for f in range(0, WIDTH, LANES):
        rows_out[f : f + LANES, :] = grad_weight_ref[f : f + LANES, :].T

    units = send_ref.shape[0]
    share = WIDTH // (2 * units)

    def pack(u, carry):
        for other, out in ((0, keep_ref), (1, send_ref)):
            panel = 2 * u + (core + other) % 2
            start = pl.multiple_of(panel * BLK, BLK)
            w_start = pl.multiple_of(panel * share, share)
            unit = jnp.concatenate(
                [
                    grad_src_ref[pl.ds(start, BLK), :],
                    rows_out[pl.ds(w_start, share), :],
                    jnp.where(panel == 0, att8, 0.0),
                ],
                axis=0,
            )
            out[u] = unit.astype(out.dtype)
        return carry

    lax.fori_loop(0, units, pack, 0)


def unpack(small_ref, grad_weight_ref, att_src_ref, att_dst_ref):
    panels = small_ref.shape[0]
    share = WIDTH // panels
    per = IN // share
    for p in range(panels):
        rows, lanes = p % per * share, p // per * LANES
        grad_weight_ref[rows : rows + share, lanes : lanes + LANES] = small_ref[p, 0:share].astype(F32)
    att = small_ref[0, share : share + 2 * WIDTH // LANES].astype(F32)
    pieces = WIDTH // LANES
    for k, out in enumerate((att_src_ref, att_dst_ref)):
        for q in range(pieces):
            line = att[k * pieces + q : k * pieces + q + 1]
            out[2 * q : 2 * q + 1, :] = line[:, :HEAD_DIM]
            out[2 * q + 1 : 2 * q + 2, :] = line[:, HEAD_DIM:]


def prep(x_dst, weight, att_src, att_dst, grad_out, block_masks):
    slots = block_masks.shape[0]
    dest = x_dst.shape[0]
    dest_blocks = dest // BLK
    att_src_row, att_dst_row = att_src.reshape(1, WIDTH), att_dst.reshape(1, WIDTH)
    params = pltpu.CompilerParams(vmem_limit_bytes=VMEM_BYTES)
    rows8 = jax.ShapeDtypeStruct((HEADS, dest), F32)
    return pl.pallas_call(
        prepare,
        out_shape=[
            jax.ShapeDtypeStruct((WIDTH, dest), BF16),
            jax.ShapeDtypeStruct((WIDTH, dest), BF16),
            jax.ShapeDtypeStruct((slots, BLK, BLK), F32),
            jax.ShapeDtypeStruct((dest_blocks, SPREAD, HEADS * BLK), BF16),
            rows8, rows8, rows8,
        ],
        compiler_params=params,
        cost_estimate=pl.CostEstimate(flops=2 * dest * IN * WIDTH, bytes_accessed=6 << 20, transcendentals=0),
        name="prepare",
    )(x_dst, weight, att_src_row, att_dst_row, grad_out, block_masks)


def local(x_own, x_other, x_dst, weight, att_src, att_dst, block_rows, block_cols, place, prepared):
    proj, grad_t, mask_t, spread, self_w, slope, pair = prepared
    slots = mask_t.shape[0]
    dest = x_dst.shape[0]
    dest_blocks = dest // BLK
    sources = 2 * x_own.shape[0]
    panels = sources // BLK
    att_src_row = att_src.reshape(1, WIDTH)
    att_src_col, att_dst_col = att_src.reshape(WIDTH, 1), att_dst.reshape(WIDTH, 1)
    params = pltpu.CompilerParams(vmem_limit_bytes=VMEM_BYTES)
    ext = 80
    operands = (
        x_own, x_other, x_dst, weight, att_src_row, att_src_col, att_dst_col,
        proj, grad_t, mask_t, spread, self_w, slope, pair,
    )
    units = panels // 2
    share = WIDTH // panels
    unit_rows = BLK + share + 8
    outs = [
        jax.ShapeDtypeStruct((dest, IN), F32),
        jax.ShapeDtypeStruct((units, unit_rows, LANES), F32),
        jax.ShapeDtypeStruct((units, unit_rows, LANES), BF16),
    ]
    return pl.pallas_call(
        edges,
        out_shape=outs,
        in_specs=[pl.BlockSpec(memory_space=pltpu.SMEM)] * 3
        + [pl.BlockSpec(memory_space=pltpu.VMEM)] * len(operands),
        out_specs=[pl.BlockSpec(memory_space=pltpu.VMEM)] * len(outs),
        scratch_shapes=[
            pltpu.VMEM((slots, WIDTH, BLK), BF16),
            pltpu.VMEM((slots, HEADS, BLK, 2 * BLK), BF16),
            pltpu.VMEM((dest_blocks, HEADS, ext, 2 * BLK), F32),
            pltpu.VMEM((dest_blocks, HEADS, ext, BLK), BF16),
            pltpu.VMEM((dest_blocks, HEADS, 8, BLK), F32),
            pltpu.VMEM((WIDTH, 32), F32),
            pltpu.VMEM((sources, IN), F32),
            pltpu.VMEM((WIDTH, IN), F32),
            pltpu.VMEM((WIDTH, IN), F32),
            pltpu.VMEM((slots, BLK, SPREAD), BF16),
            pltpu.VMEM((WIDTH, LANES), F32),
            pltpu.VMEM((sources, IN), BF16),
        ],
        compiler_params=params,
        cost_estimate=pl.CostEstimate(flops=4 << 30, bytes_accessed=12 << 20, transcendentals=8 << 20),
        name="edges",
    )(block_rows, block_cols, place, *operands)


def shards(
    x_src, x_dst, weight, att_src, att_dst, grad_out, block_rows, block_cols, block_masks, block_counts
):
    panels = lax.axis_size("panel")
    units = panels // 2
    share = WIDTH // panels
    same_core = [[p for p in range(panels) if p % 2 == core] for core in range(2)]
    siblings = [(p, p ^ 1) for p in range(panels)]

    def spread(values, axis, count, groups=None):
        return lax.all_to_all(
            jnp.broadcast_to(values[None], (count, *values.shape)), axis, 0, 0, axis_index_groups=groups
        )

    x_own = spread(x_src, "panel", units, same_core).reshape(-1, IN)
    prepared = prep(x_dst, weight, att_src, att_dst, grad_out, block_masks)
    x_own, prepared = lax.optimization_barrier((x_own, prepared))
    x_other = lax.ppermute(x_own, "panel", siblings)
    place = lax.axis_index("panel").reshape(1)
    grad_dst, keep, send = local(
        x_own, x_other, x_dst, weight, att_src, att_dst, block_rows, block_cols, place, prepared
    )
    half = (keep + lax.ppermute(send, "panel", siblings).astype(F32)).astype(BF16)
    got = lax.all_to_all(half, "panel", 0, 0, axis_index_groups=same_core)
    unit = got.astype(F32).sum(axis=0).astype(BF16)
    reps = lax.axis_size("rep")
    part, small = unit[:BLK], unit[BLK:]
    bit = 1
    while bit < reps:
        other = lax.ppermute(part, "rep", [(i, i ^ bit) for i in range(reps)])
        grad_src = part.astype(F32) + other.astype(F32)
        part = grad_src.astype(BF16)
        bit *= 2
    small = spread(small, "rep", reps).astype(F32).sum(axis=0).astype(BF16)
    small = spread(small, "panel", panels)
    grad_weight, grad_att_src, grad_att_dst = pl.pallas_call(
        unpack,
        out_shape=[
            jax.ShapeDtypeStruct((IN, WIDTH), F32),
            jax.ShapeDtypeStruct((HEADS, HEAD_DIM), F32),
            jax.ShapeDtypeStruct((HEADS, HEAD_DIM), F32),
        ],
        name="unpack",
    )(small)
    return grad_src, grad_dst, grad_weight, grad_att_src, grad_att_dst


def solution(mesh):
    return jax.shard_map(
        shards,
        mesh=mesh,
        in_specs=(
            P("panel", None),
            P(("panel", "rep"), None),
            P(),
            P(),
            P(),
            P(("panel", "rep"), None),
            P(("panel", "rep")),
            P(("panel", "rep")),
            P(("panel", "rep"), None, None),
            P(("panel", "rep")),
        ),
        out_specs=(P("panel", None), P(("panel", "rep"), None), P(), P(), P()),
        check_vma=False,
    )
```

```python
import jax
import jax.numpy as jnp
from jax import lax
from jax.experimental import pallas as pl
from jax.experimental.pallas import tpu as pltpu
from jax.sharding import PartitionSpec as P

HEADS, HEAD_DIM, IN, WIDTH, BLK = 8, 64, 128, 512, 128
LOG2E = 1.4426950408889634
LANES = 128
F32, BF16 = jnp.float32, jnp.bfloat16
VMEM_BYTES = 40 << 20

NN = (((1,), (0,)), ((), ()))
NT = (((1,), (1,)), ((), ()))
TN = (((0,), (0,)), ((), ()))


def mm(a, b, dims=NN):
    return lax.dot_general(a, b, dims, preferred_element_type=F32)


def split2(values):
    hi = values.astype(BF16)
    return hi, (values - hi.astype(F32)).astype(BF16)


def split3(values):
    hi = values.astype(BF16)
    rest = values - hi.astype(F32)
    mid = rest.astype(BF16)
    return hi, mid, (rest - mid.astype(F32)).astype(BF16)


def head_rows(att_flat):
    head = lax.broadcasted_iota(jnp.int32, (HEADS, WIDTH), 0)
    lane = lax.broadcasted_iota(jnp.int32, (HEADS, WIDTH), 1) // HEAD_DIM
    return jnp.where(head == lane, jnp.broadcast_to(att_flat, (HEADS, WIDTH)), 0.0)


def per_head(rows):
    width = rows.shape[1]
    return jnp.concatenate(
        [jnp.broadcast_to(rows[h : h + 1], (HEAD_DIM, width)) for h in range(HEADS)], axis=0
    )


def head_sums(values):
    return jnp.concatenate(
        [
            jnp.sum(values[h * HEAD_DIM : (h + 1) * HEAD_DIM], axis=0, keepdims=True)
            for h in range(HEADS)
        ],
        axis=0,
    )


def weight_and_slope(pre2):
    log = jnp.log2(1.0 + jnp.exp2(pre2))
    return jnp.exp2(0.2 * pre2 + 0.8 * log), 1.0 - 0.8 * jnp.exp2(-log)


def prepare(
    x_dst_ref, weight_ref, att_src_ref, att_dst_ref, grad_ref, mask_ref,
    proj_ref, grad_t_ref, mask_t_ref, score_ref, self_ref, slope_ref, pair_ref,
):
    weight_t = weight_ref[...].astype(F32).T.astype(BF16)
    proj = mm(weight_t, x_dst_ref[...], NT).astype(BF16)
    proj_ref[...] = proj
    grad_t = grad_ref[...].astype(F32).T
    grad_t_ref[...] = grad_t.astype(BF16)
    parts = split3(head_rows(att_dst_ref[...])) + split3(head_rows(att_src_ref[...]))
    scores = mm(jnp.concatenate(parts, axis=0), proj)
    score_d = (scores[0:8] + scores[8:16]) + scores[16:24]
    score_own = (scores[24:32] + scores[32:40]) + scores[40:48]
    for r in range(score_ref.shape[0]):
        score_ref[r] = score_d[:, r * BLK : (r + 1) * BLK] * LOG2E
    weight_self, slope_self = weight_and_slope((score_d + score_own) * LOG2E)
    self_ref[...] = weight_self
    slope_ref[...] = slope_self
    pair_ref[...] = head_sums(grad_t * proj.astype(F32))

    def turn(b, carry):
        mask_t_ref[b] = mask_ref[b].astype(F32).T
        return carry

    lax.fori_loop(0, mask_ref.shape[0], turn, 0)


def edges(
    rows_ref, cols_ref, place_ref,
    x_own_ref, x_other_ref, x_dst_ref, weight_ref, att_src_ref, att_src_col_ref, att_dst_col_ref,
    proj_ref, grad_t_ref, mask_t_ref, score_ref, self_ref, slope_ref, pair_ref,
    grad_dst_ref, keep_ref, send_ref,
    proj_src, tiles, acc, scaled, scaled_c, own, grad_src_ref, grad_weight_ref, rows_out, score_cols, att_wide, x_all,
):
    slots = mask_t_ref.shape[0]
    dest_blocks = acc.shape[0]
    ext = acc.shape[2]
    weight = weight_ref[...]
    weight_t = weight.astype(F32).T.astype(BF16)
    att_rows = jnp.concatenate(split3(head_rows(att_src_ref[...])), axis=0)
    acc[...] = jnp.zeros(acc.shape, F32)
    grad_src_ref[...] = jnp.zeros(grad_src_ref.shape, grad_src_ref.dtype)
    ones = jnp.ones((ext - HEAD_DIM, BLK), BF16)

    att_wide[...] = jnp.broadcast_to(att_src_col_ref[...], att_wide.shape)

    core = place_ref[0] % 2
    half = x_own_ref.shape[0]
    x_all[0:half] = x_own_ref[...]
    x_all[half : 2 * half] = x_other_ref[...]

    def block(b):
        return pl.ds(pl.multiple_of(cols_ref[b] * BLK, BLK), BLK)

    def sources(b):
        col = cols_ref[b]
        place = (col % 2 + core) % 2 * half + col // 2 * BLK
        return x_all[pl.ds(pl.multiple_of(place, BLK), BLK), :]

    group = jnp.concatenate([sources(b) for b in range(slots)], axis=0)
    projs = mm(weight_t, group, NT).astype(BF16)
    scores = mm(att_rows, projs)
    score_t = (((scores[0:8] + scores[8:16]) + scores[16:24]) * LOG2E).T
    for b in range(slots):
        proj_src[b] = projs[:, b * BLK : (b + 1) * BLK]
        score_cols[b] = score_t[b * BLK : (b + 1) * BLK]

    def forward(b, carry):
        row = rows_ref[b]
        proj = proj_src[b]
        cols = score_cols[b]
        mask = mask_t_ref[b]
        score_d = score_ref[row]
        for h in range(HEADS):
            pre2 = jnp.broadcast_to(cols[:, h : h + 1], (BLK, BLK)) + score_d[h : h + 1]
            weight_e, slope = weight_and_slope(pre2)
            weight_e = weight_e * mask
            pair = jnp.concatenate(
                [weight_e.astype(BF16), (weight_e * slope).astype(BF16)], axis=1
            )
            tiles[b, h] = pair
            left = jnp.concatenate([proj[h * HEAD_DIM : (h + 1) * HEAD_DIM], ones], axis=0)
            acc[row, h] += mm(left, pair)
        return carry

    lax.fori_loop(0, slots, forward, 0, unroll=4)

    self_att_rows, self_grad_rows, grad_d_rows = [], [], []
    for r in range(dest_blocks):
        lanes = slice(r * BLK, (r + 1) * BLK)
        self_w = self_ref[:, lanes]
        selfs, grads, dsts = [], [], []
        for h in range(HEADS):
            feats = slice(h * HEAD_DIM, (h + 1) * HEAD_DIM)
            sums = acc[r, h]
            w_self = self_w[h : h + 1]
            inv = 1.0 / (sums[HEAD_DIM : HEAD_DIM + 1, :BLK] + w_self)
            numer = sums[:HEAD_DIM, :BLK] + w_self * proj_ref[feats, lanes].astype(F32)
            grad = grad_t_ref[feats, lanes].astype(F32)
            part = (grad * inv).astype(BF16)
            part_wide = part.astype(F32)
            centred = jnp.sum(grad * numer, axis=0, keepdims=True) * inv
            centred_part = jnp.sum(part_wide * numer, axis=0, keepdims=True) * inv
            grad_d = (
                jnp.sum(part_wide * sums[:HEAD_DIM, BLK:], axis=0, keepdims=True)
                - centred_part * sums[HEAD_DIM : HEAD_DIM + 1, BLK:]
            )
            att_self = w_self * inv
            grad_self = (
                att_self * (pair_ref[h : h + 1, lanes] - centred) * slope_ref[h : h + 1, lanes]
            )
            scaled[r, h, 0:HEAD_DIM] = part
            c_hi, c_lo = split2(centred_part)
            scaled_c[r, h, 0:1] = c_hi.astype(F32)
            scaled_c[r, h, 1:2] = c_lo.astype(F32)
            selfs.append(att_self)
            grads.append(grad_self)
            dsts.append(grad_d + grad_self)
        self_att_rows.append(jnp.concatenate(selfs, axis=0))
        self_grad_rows.append(jnp.concatenate(grads, axis=0))
        grad_d_rows.append(jnp.concatenate(dsts, axis=0))
    for r in range(dest_blocks):
        for h in range(HEADS):
            scaled[r, h, HEAD_DIM:ext] = jnp.concatenate(
                [scaled_c[r, h, 0:2], jnp.zeros((ext - HEAD_DIM - 2, BLK), F32)], axis=0
            ).astype(BF16)

    att_src_wide = att_wide[...]
    att_dst_wide = jnp.broadcast_to(att_dst_col_ref[...], att_wide.shape)
    grad_weight = jnp.zeros((WIDTH, IN), F32)
    att_sums = jnp.zeros((WIDTH, 32), F32)
    for r in range(dest_blocks):
        lanes = slice(r * BLK, (r + 1) * BLK)
        grad_proj = (
            per_head(self_att_rows[r]) * grad_t_ref[:, lanes].astype(F32)
            + per_head(self_grad_rows[r]) * att_src_wide
            + per_head(grad_d_rows[r]) * att_dst_wide
        ).astype(BF16)
        grad_dst_ref[lanes, :] = mm(weight, grad_proj).T
        grad_weight = grad_weight + mm(grad_proj, x_dst_ref[lanes, :])
        both = jnp.concatenate(split2(self_grad_rows[r]) + split2(grad_d_rows[r]), axis=0)
        att_sums = att_sums + mm(proj_ref[:, lanes], both, NT)
    grad_weight_ref[...] = grad_weight
    own[...] = att_sums

    def back(b):
        row = rows_ref[b]
        proj = proj_src[b]
        feats, grads = [], []
        for h in range(HEADS):
            pair = tiles[b, h]
            stack = jnp.concatenate([pair[:, :BLK], pair[:, BLK:]], axis=0)
            out = mm(scaled[row, h], stack, NT)
            feats.append(out[:HEAD_DIM, :BLK])
            proj_h = proj[h * HEAD_DIM : (h + 1) * HEAD_DIM].astype(F32)
            grads.append(
                jnp.sum(proj_h * out[:HEAD_DIM, BLK:], axis=0, keepdims=True)
                - (out[HEAD_DIM : HEAD_DIM + 1, BLK:] + out[HEAD_DIM + 1 : HEAD_DIM + 2, BLK:])
            )
        grad_s = jnp.concatenate(grads, axis=0)
        grad_proj = jnp.concatenate(feats, axis=0) + per_head(grad_s) * att_wide[...]
        return proj, grad_s, grad_proj.astype(BF16)

    def backward(step, carry):
        b = 2 * step
        projs, grads, parts = zip(back(b), back(b + 1))
        grad_proj = jnp.concatenate(parts, axis=1)
        into = mm(weight, grad_proj)
        x_pair = jnp.concatenate([sources(b), sources(b + 1)], axis=0)
        grad_weight_ref[...] += mm(grad_proj, x_pair)
        grad_s = jnp.concatenate(split2(jnp.concatenate(grads, axis=1)), axis=0)
        own[:, 0:16] += mm(jnp.concatenate(projs, axis=1), grad_s, NT)
        for k in range(2):
            grad_src_ref[block(b + k), :] += into[:, k * BLK : (k + 1) * BLK].T
        return carry

    lax.fori_loop(0, slots // 2, backward, 0, unroll=8)

    sums = own[...]
    head = lax.broadcasted_iota(jnp.int32, (WIDTH, HEADS), 1)
    feat = lax.broadcasted_iota(jnp.int32, (WIDTH, HEADS), 0) // HEAD_DIM
    pick = head == feat
    src = jnp.where(pick, sums[:, 0:8] + sums[:, 8:16], 0.0)
    dst = jnp.where(pick, sums[:, 16:24] + sums[:, 24:32], 0.0)
    att_rows8 = [
        jnp.sum(part[f : f + LANES].T, axis=0, keepdims=True)
        for part in (src, dst)
        for f in range(0, WIDTH, LANES)
    ]
    att8 = jnp.concatenate(att_rows8, axis=0)
    for f in range(0, WIDTH, LANES):
        rows_out[f : f + LANES, :] = grad_weight_ref[f : f + LANES, :].T

    units = send_ref.shape[0]
    share = WIDTH // (2 * units)

    def pack(u, carry):
        for other, out in ((0, keep_ref), (1, send_ref)):
            panel = 2 * u + (core + other) % 2
            start = pl.multiple_of(panel * BLK, BLK)
            w_start = pl.multiple_of(panel * share, share)
            unit = jnp.concatenate(
                [
                    grad_src_ref[pl.ds(start, BLK), :],
                    rows_out[pl.ds(w_start, share), :],
                    jnp.where(panel == 0, att8, 0.0),
                ],
                axis=0,
            )
            out[u] = unit.astype(out.dtype)
        return carry

    lax.fori_loop(0, units, pack, 0)


def prep(x_dst, weight, att_src, att_dst, grad_out, block_masks):
    slots = block_masks.shape[0]
    dest = x_dst.shape[0]
    dest_blocks = dest // BLK
    att_src_row, att_dst_row = att_src.reshape(1, WIDTH), att_dst.reshape(1, WIDTH)
    params = pltpu.CompilerParams(vmem_limit_bytes=VMEM_BYTES)
    rows8 = jax.ShapeDtypeStruct((HEADS, dest), F32)
    return pl.pallas_call(
        prepare,
        out_shape=[
            jax.ShapeDtypeStruct((WIDTH, dest), BF16),
            jax.ShapeDtypeStruct((WIDTH, dest), BF16),
            jax.ShapeDtypeStruct((slots, BLK, BLK), F32),
            jax.ShapeDtypeStruct((dest_blocks, HEADS, BLK), F32),
            rows8, rows8, rows8,
        ],
        compiler_params=params,
        cost_estimate=pl.CostEstimate(flops=2 * dest * IN * WIDTH, bytes_accessed=6 << 20, transcendentals=0),
        name="prepare",
    )(x_dst, weight, att_src_row, att_dst_row, grad_out, block_masks)


def local(x_own, x_other, x_dst, weight, att_src, att_dst, block_rows, block_cols, place, prepared):
    proj, grad_t, mask_t, score, self_w, slope, pair = prepared
    slots = mask_t.shape[0]
    dest = x_dst.shape[0]
    dest_blocks = dest // BLK
    sources = 2 * x_own.shape[0]
    panels = sources // BLK
    att_src_row = att_src.reshape(1, WIDTH)
    att_src_col, att_dst_col = att_src.reshape(WIDTH, 1), att_dst.reshape(WIDTH, 1)
    params = pltpu.CompilerParams(vmem_limit_bytes=VMEM_BYTES)
    ext = 80
    operands = (
        x_own, x_other, x_dst, weight, att_src_row, att_src_col, att_dst_col,
        proj, grad_t, mask_t, score, self_w, slope, pair,
    )
    units = panels // 2
    share = WIDTH // panels
    unit_rows = BLK + share + 8
    outs = [
        jax.ShapeDtypeStruct((dest, IN), F32),
        jax.ShapeDtypeStruct((units, unit_rows, LANES), F32),
        jax.ShapeDtypeStruct((units, unit_rows, LANES), BF16),
    ]
    return pl.pallas_call(
        edges,
        out_shape=outs,
        in_specs=[pl.BlockSpec(memory_space=pltpu.SMEM)] * 3
        + [pl.BlockSpec(memory_space=pltpu.VMEM)] * len(operands),
        out_specs=[pl.BlockSpec(memory_space=pltpu.VMEM)] * len(outs),
        scratch_shapes=[
            pltpu.VMEM((slots, WIDTH, BLK), BF16),
            pltpu.VMEM((slots, HEADS, BLK, 2 * BLK), BF16),
            pltpu.VMEM((dest_blocks, HEADS, ext, 2 * BLK), F32),
            pltpu.VMEM((dest_blocks, HEADS, ext, BLK), BF16),
            pltpu.VMEM((dest_blocks, HEADS, 8, BLK), F32),
            pltpu.VMEM((WIDTH, 32), F32),
            pltpu.VMEM((sources, IN), F32),
            pltpu.VMEM((WIDTH, IN), F32),
            pltpu.VMEM((WIDTH, IN), F32),
            pltpu.VMEM((slots, BLK, HEADS), F32),
            pltpu.VMEM((WIDTH, LANES), F32),
            pltpu.VMEM((sources, IN), BF16),
        ],
        compiler_params=params,
        cost_estimate=pl.CostEstimate(flops=4 << 30, bytes_accessed=12 << 20, transcendentals=8 << 20),
        name="edges",
    )(block_rows, block_cols, place, *operands)


def shards(
    x_src, x_dst, weight, att_src, att_dst, grad_out, block_rows, block_cols, block_masks, block_counts
):
    panels = lax.axis_size("panel")
    units = panels // 2
    share = WIDTH // panels
    same_core = [[p for p in range(panels) if p % 2 == core] for core in range(2)]
    siblings = [(p, p ^ 1) for p in range(panels)]

    def spread(values, axis, count, groups=None):
        return lax.all_to_all(
            jnp.broadcast_to(values[None], (count, *values.shape)), axis, 0, 0, axis_index_groups=groups
        )

    x_own = spread(x_src, "panel", units, same_core).reshape(-1, IN)
    prepared = prep(x_dst, weight, att_src, att_dst, grad_out, block_masks)
    x_own, slope = lax.optimization_barrier((x_own, prepared[5]))
    prepared = [*prepared[:5], slope, *prepared[6:]]
    x_other = lax.ppermute(x_own, "panel", siblings)
    place = lax.axis_index("panel").reshape(1)
    grad_dst, keep, send = local(
        x_own, x_other, x_dst, weight, att_src, att_dst, block_rows, block_cols, place, prepared
    )
    half = (keep + lax.ppermute(send, "panel", siblings).astype(F32)).astype(BF16)
    got = lax.all_to_all(half, "panel", 0, 0, axis_index_groups=same_core)
    unit = got.astype(F32).sum(axis=0).astype(BF16)
    total = spread(unit, "rep", lax.axis_size("rep")).astype(F32).sum(axis=0)
    grad_src = total[:BLK]
    small = spread(total[BLK:].astype(BF16), "panel", panels).astype(F32)
    grad_weight = small[:, :share].reshape(WIDTH // LANES, IN, LANES).transpose(1, 0, 2).reshape(IN, WIDTH)
    att = small[0, share:].reshape(2, HEADS, HEAD_DIM)
    return grad_src, grad_dst, grad_weight, att[0], att[1]


def solution(mesh):
    return jax.shard_map(
        shards,
        mesh=mesh,
        in_specs=(
            P("panel", None),
            P(("panel", "rep"), None),
            P(),
            P(),
            P(),
            P(("panel", "rep"), None),
            P(("panel", "rep")),
            P(("panel", "rep")),
            P(("panel", "rep"), None, None),
            P(("panel", "rep")),
        ),
        out_specs=(P("panel", None), P(("panel", "rep"), None), P(), P(), P()),
        check_vma=False,
    )
```

```python
import jax
import jax.numpy as jnp
from jax import lax
from jax.experimental import pallas as pl
from jax.experimental.pallas import tpu as pltpu
from jax.sharding import PartitionSpec as P

HEADS, HEAD_DIM, IN, WIDTH, BLK = 8, 64, 128, 512, 128
LOG2E = 1.4426950408889634
LANES = 128
F32, BF16 = jnp.float32, jnp.bfloat16
VMEM_BYTES = 40 << 20

NN = (((1,), (0,)), ((), ()))
NT = (((1,), (1,)), ((), ()))
TN = (((0,), (0,)), ((), ()))


def mm(a, b, dims=NN):
    return lax.dot_general(a, b, dims, preferred_element_type=F32)


def split2(values):
    hi = values.astype(BF16)
    return hi, (values - hi.astype(F32)).astype(BF16)


def split3(values):
    hi = values.astype(BF16)
    rest = values - hi.astype(F32)
    mid = rest.astype(BF16)
    return hi, mid, (rest - mid.astype(F32)).astype(BF16)


def head_rows(att):
    head = lax.broadcasted_iota(jnp.int32, (HEADS, WIDTH), 0)
    lane = lax.broadcasted_iota(jnp.int32, (HEADS, WIDTH), 1) // HEAD_DIM
    return jnp.where(head == lane, jnp.concatenate([att] * HEADS, axis=1), 0.0)


def feature_rows(att):
    flat = jnp.sum(head_rows(att), axis=0, keepdims=True)
    return jnp.broadcast_to(flat, (LANES, WIDTH)).T


def per_head(rows):
    width = rows.shape[1]
    return jnp.concatenate(
        [jnp.broadcast_to(rows[h : h + 1], (HEAD_DIM, width)) for h in range(HEADS)], axis=0
    )


def head_sums(values):
    return jnp.concatenate(
        [
            jnp.sum(values[h * HEAD_DIM : (h + 1) * HEAD_DIM], axis=0, keepdims=True)
            for h in range(HEADS)
        ],
        axis=0,
    )


def weight_and_slope(pre2):
    log = jnp.log2(1.0 + jnp.exp2(pre2))
    return jnp.exp2(0.2 * pre2 + 0.8 * log), 1.0 - 0.8 * jnp.exp2(-log)


def prepare(
    x_dst_ref, weight_ref, att_src_ref, att_dst_ref, grad_ref, mask_ref,
    proj_ref, grad_t_ref, mask_t_ref, score_ref, self_ref, slope_ref, pair_ref,
):
    weight_t = weight_ref[...].astype(F32).T.astype(BF16)
    proj = mm(weight_t, x_dst_ref[...], NT).astype(BF16)
    proj_ref[...] = proj
    grad_t = grad_ref[...].astype(F32).T
    grad_t_ref[...] = grad_t.astype(BF16)
    parts = split3(head_rows(att_dst_ref[...])) + split3(head_rows(att_src_ref[...]))
    scores = mm(jnp.concatenate(parts, axis=0), proj)
    score_d = (scores[0:8] + scores[8:16]) + scores[16:24]
    score_own = (scores[24:32] + scores[32:40]) + scores[40:48]
    for r in range(score_ref.shape[0]):
        score_ref[r] = score_d[:, r * BLK : (r + 1) * BLK] * LOG2E
    weight_self, slope_self = weight_and_slope((score_d + score_own) * LOG2E)
    self_ref[...] = weight_self
    slope_ref[...] = slope_self
    pair_ref[...] = head_sums(grad_t * proj.astype(F32))

    def turn(b, carry):
        mask_t_ref[b] = mask_ref[b].astype(F32).T
        return carry

    lax.fori_loop(0, mask_ref.shape[0], turn, 0)


def edges(
    rows_ref, cols_ref, place_ref,
    x_own_ref, x_other_ref, x_dst_ref, weight_ref, att_src_ref, att_dst_ref,
    proj_ref, grad_t_ref, mask_t_ref, score_ref, self_ref, slope_ref, pair_ref,
    grad_dst_ref, keep_ref, send_ref,
    proj_src, tiles, acc, scaled, scaled_c, own, grad_src_ref, grad_weight_ref, rows_out, score_cols, att_wide, x_all,
):
    slots = mask_t_ref.shape[0]
    dest_blocks = acc.shape[0]
    ext = acc.shape[2]
    weight = weight_ref[...]
    weight_t = weight.astype(F32).T.astype(BF16)
    att_rows = jnp.concatenate(split3(head_rows(att_src_ref[...])), axis=0)
    acc[...] = jnp.zeros(acc.shape, F32)
    grad_src_ref[...] = jnp.zeros(grad_src_ref.shape, grad_src_ref.dtype)
    ones = jnp.ones((ext - HEAD_DIM, BLK), BF16)

    att_wide[...] = feature_rows(att_src_ref[...])

    core = place_ref[0] % 2
    half = x_own_ref.shape[0]
    x_all[0:half] = x_own_ref[...]
    x_all[half : 2 * half] = x_other_ref[...]

    def block(b):
        return pl.ds(pl.multiple_of(cols_ref[b] * BLK, BLK), BLK)

    def sources(b):
        col = cols_ref[b]
        place = (col % 2 + core) % 2 * half + col // 2 * BLK
        return x_all[pl.ds(pl.multiple_of(place, BLK), BLK), :]

    group = jnp.concatenate([sources(b) for b in range(slots)], axis=0)
    projs = mm(weight_t, group, NT).astype(BF16)
    scores = mm(att_rows, projs)
    score_t = (((scores[0:8] + scores[8:16]) + scores[16:24]) * LOG2E).T
    for b in range(slots):
        proj_src[b] = projs[:, b * BLK : (b + 1) * BLK]
        score_cols[b] = score_t[b * BLK : (b + 1) * BLK]

    def forward(b, carry):
        row = rows_ref[b]
        proj = proj_src[b]
        cols = score_cols[b]
        mask = mask_t_ref[b]
        score_d = score_ref[row]
        for h in range(HEADS):
            pre2 = jnp.broadcast_to(cols[:, h : h + 1], (BLK, BLK)) + score_d[h : h + 1]
            weight_e, slope = weight_and_slope(pre2)
            weight_e = weight_e * mask
            pair = jnp.concatenate(
                [weight_e.astype(BF16), (weight_e * slope).astype(BF16)], axis=1
            )
            tiles[b, h] = pair
            left = jnp.concatenate([proj[h * HEAD_DIM : (h + 1) * HEAD_DIM], ones], axis=0)
            acc[row, h] += mm(left, pair)
        return carry

    lax.fori_loop(0, slots, forward, 0, unroll=4)

    self_att_rows, self_grad_rows, grad_d_rows = [], [], []
    for r in range(dest_blocks):
        lanes = slice(r * BLK, (r + 1) * BLK)
        self_w = self_ref[:, lanes]
        selfs, grads, dsts = [], [], []
        for h in range(HEADS):
            feats = slice(h * HEAD_DIM, (h + 1) * HEAD_DIM)
            sums = acc[r, h]
            w_self = self_w[h : h + 1]
            inv = 1.0 / (sums[HEAD_DIM : HEAD_DIM + 1, :BLK] + w_self)
            numer = sums[:HEAD_DIM, :BLK] + w_self * proj_ref[feats, lanes].astype(F32)
            grad = grad_t_ref[feats, lanes].astype(F32)
            part = (grad * inv).astype(BF16)
            part_wide = part.astype(F32)
            centred = jnp.sum(grad * numer, axis=0, keepdims=True) * inv
            centred_part = jnp.sum(part_wide * numer, axis=0, keepdims=True) * inv
            grad_d = (
                jnp.sum(part_wide * sums[:HEAD_DIM, BLK:], axis=0, keepdims=True)
                - centred_part * sums[HEAD_DIM : HEAD_DIM + 1, BLK:]
            )
            att_self = w_self * inv
            grad_self = (
                att_self * (pair_ref[h : h + 1, lanes] - centred) * slope_ref[h : h + 1, lanes]
            )
            scaled[r, h, 0:HEAD_DIM] = part
            c_hi, c_lo = split2(centred_part)
            scaled_c[r, h, 0:1] = c_hi.astype(F32)
            scaled_c[r, h, 1:2] = c_lo.astype(F32)
            selfs.append(att_self)
            grads.append(grad_self)
            dsts.append(grad_d + grad_self)
        self_att_rows.append(jnp.concatenate(selfs, axis=0))
        self_grad_rows.append(jnp.concatenate(grads, axis=0))
        grad_d_rows.append(jnp.concatenate(dsts, axis=0))
    for r in range(dest_blocks):
        for h in range(HEADS):
            scaled[r, h, HEAD_DIM:ext] = jnp.concatenate(
                [scaled_c[r, h, 0:2], jnp.zeros((ext - HEAD_DIM - 2, BLK), F32)], axis=0
            ).astype(BF16)

    att_src_wide = att_wide[...]
    att_dst_wide = feature_rows(att_dst_ref[...])
    grad_weight = jnp.zeros((WIDTH, IN), F32)
    att_sums = jnp.zeros((WIDTH, 32), F32)
    for r in range(dest_blocks):
        lanes = slice(r * BLK, (r + 1) * BLK)
        grad_proj = (
            per_head(self_att_rows[r]) * grad_t_ref[:, lanes].astype(F32)
            + per_head(self_grad_rows[r]) * att_src_wide
            + per_head(grad_d_rows[r]) * att_dst_wide
        ).astype(BF16)
        grad_dst_ref[lanes, :] = mm(weight, grad_proj).T
        grad_weight = grad_weight + mm(grad_proj, x_dst_ref[lanes, :])
        both = jnp.concatenate(split2(self_grad_rows[r]) + split2(grad_d_rows[r]), axis=0)
        att_sums = att_sums + mm(proj_ref[:, lanes], both, NT)
    grad_weight_ref[...] = grad_weight
    own[...] = att_sums

    def back(b):
        row = rows_ref[b]
        proj = proj_src[b]
        feats, grads = [], []
        for h in range(HEADS):
            pair = tiles[b, h]
            stack = jnp.concatenate([pair[:, :BLK], pair[:, BLK:]], axis=0)
            out = mm(scaled[row, h], stack, NT)
            feats.append(out[:HEAD_DIM, :BLK])
            proj_h = proj[h * HEAD_DIM : (h + 1) * HEAD_DIM].astype(F32)
            grads.append(
                jnp.sum(proj_h * out[:HEAD_DIM, BLK:], axis=0, keepdims=True)
                - (out[HEAD_DIM : HEAD_DIM + 1, BLK:] + out[HEAD_DIM + 1 : HEAD_DIM + 2, BLK:])
            )
        grad_s = jnp.concatenate(grads, axis=0)
        grad_proj = jnp.concatenate(feats, axis=0) + per_head(grad_s) * att_wide[...]
        return proj, grad_s, grad_proj.astype(BF16)

    def backward(step, carry):
        b = 2 * step
        projs, grads, parts = zip(back(b), back(b + 1))
        grad_proj = jnp.concatenate(parts, axis=1)
        into = mm(weight, grad_proj)
        x_pair = jnp.concatenate([sources(b), sources(b + 1)], axis=0)
        grad_weight_ref[...] += mm(grad_proj, x_pair)
        grad_s = jnp.concatenate(split2(jnp.concatenate(grads, axis=1)), axis=0)
        own[:, 0:16] += mm(jnp.concatenate(projs, axis=1), grad_s, NT)
        for k in range(2):
            grad_src_ref[block(b + k), :] += into[:, k * BLK : (k + 1) * BLK].T
        return carry

    lax.fori_loop(0, slots // 2, backward, 0, unroll=8)

    sums = own[...]
    head = lax.broadcasted_iota(jnp.int32, (WIDTH, HEADS), 1)
    feat = lax.broadcasted_iota(jnp.int32, (WIDTH, HEADS), 0) // HEAD_DIM
    pick = head == feat
    src = jnp.where(pick, sums[:, 0:8] + sums[:, 8:16], 0.0)
    dst = jnp.where(pick, sums[:, 16:24] + sums[:, 24:32], 0.0)
    low = lax.broadcasted_iota(jnp.int32, (HEADS, LANES), 1) < HEAD_DIM
    folded = []
    for part in (src, dst):
        part = part.T
        pair = sum(part[:, f : f + LANES] for f in range(0, WIDTH, LANES))
        folded.append(pair + pltpu.roll(pair, HEAD_DIM, axis=1))
    att8 = jnp.where(low, folded[0], folded[1])
    for f in range(0, WIDTH, LANES):
        rows_out[f : f + LANES, :] = grad_weight_ref[f : f + LANES, :].T

    units = send_ref.shape[0]
    share = WIDTH // (2 * units)

    def pack(u, carry):
        for other, out in ((0, keep_ref), (1, send_ref)):
            panel = 2 * u + (core + other) % 2
            start = pl.multiple_of(panel * BLK, BLK)
            w_start = pl.multiple_of(panel * share, share)
            unit = jnp.concatenate(
                [
                    grad_src_ref[pl.ds(start, BLK), :],
                    rows_out[pl.ds(w_start, share), :],
                    jnp.where(panel == 0, att8, 0.0),
                ],
                axis=0,
            )
            out[u] = unit.astype(out.dtype)
        return carry

    lax.fori_loop(0, units, pack, 0)


def prep(x_dst, weight, att_src, att_dst, grad_out, block_masks):
    slots = block_masks.shape[0]
    dest = x_dst.shape[0]
    dest_blocks = dest // BLK
    params = pltpu.CompilerParams(vmem_limit_bytes=VMEM_BYTES)
    rows8 = jax.ShapeDtypeStruct((HEADS, dest), F32)
    return pl.pallas_call(
        prepare,
        out_shape=[
            jax.ShapeDtypeStruct((WIDTH, dest), BF16),
            jax.ShapeDtypeStruct((WIDTH, dest), BF16),
            jax.ShapeDtypeStruct((slots, BLK, BLK), F32),
            jax.ShapeDtypeStruct((dest_blocks, HEADS, BLK), F32),
            rows8, rows8, rows8,
        ],
        compiler_params=params,
        cost_estimate=pl.CostEstimate(flops=2 * dest * IN * WIDTH, bytes_accessed=6 << 20, transcendentals=0),
        name="prepare",
    )(x_dst, weight, att_src, att_dst, grad_out, block_masks)


def local(x_own, x_other, x_dst, weight, att_src, att_dst, block_rows, block_cols, place, prepared):
    proj, grad_t, mask_t, score, self_w, slope, pair = prepared
    slots = mask_t.shape[0]
    dest = x_dst.shape[0]
    dest_blocks = dest // BLK
    sources = 2 * x_own.shape[0]
    panels = sources // BLK
    params = pltpu.CompilerParams(vmem_limit_bytes=VMEM_BYTES)
    ext = 80
    operands = (
        x_own, x_other, x_dst, weight, att_src, att_dst,
        proj, grad_t, mask_t, score, self_w, slope, pair,
    )
    units = panels // 2
    share = WIDTH // panels
    unit_rows = BLK + share + 8
    outs = [
        jax.ShapeDtypeStruct((dest, IN), F32),
        jax.ShapeDtypeStruct((units, unit_rows, LANES), F32),
        jax.ShapeDtypeStruct((units, unit_rows, LANES), BF16),
    ]
    return pl.pallas_call(
        edges,
        out_shape=outs,
        in_specs=[pl.BlockSpec(memory_space=pltpu.SMEM)] * 3
        + [pl.BlockSpec(memory_space=pltpu.VMEM)] * len(operands),
        out_specs=[pl.BlockSpec(memory_space=pltpu.VMEM)] * len(outs),
        scratch_shapes=[
            pltpu.VMEM((slots, WIDTH, BLK), BF16),
            pltpu.VMEM((slots, HEADS, BLK, 2 * BLK), BF16),
            pltpu.VMEM((dest_blocks, HEADS, ext, 2 * BLK), F32),
            pltpu.VMEM((dest_blocks, HEADS, ext, BLK), BF16),
            pltpu.VMEM((dest_blocks, HEADS, 8, BLK), F32),
            pltpu.VMEM((WIDTH, 32), F32),
            pltpu.VMEM((sources, IN), F32),
            pltpu.VMEM((WIDTH, IN), F32),
            pltpu.VMEM((WIDTH, IN), F32),
            pltpu.VMEM((slots, BLK, HEADS), F32),
            pltpu.VMEM((WIDTH, LANES), F32),
            pltpu.VMEM((sources, IN), BF16),
        ],
        compiler_params=params,
        cost_estimate=pl.CostEstimate(flops=4 << 30, bytes_accessed=12 << 20, transcendentals=8 << 20),
        name="edges",
    )(block_rows, block_cols, place, *operands)


def shards(
    x_src, x_dst, weight, att_src, att_dst, grad_out, block_rows, block_cols, block_masks, block_counts
):
    panels = lax.axis_size("panel")
    units = panels // 2
    share = WIDTH // panels
    same_core = [[p for p in range(panels) if p % 2 == core] for core in range(2)]
    siblings = [(p, p ^ 1) for p in range(panels)]

    def spread(values, axis, count, groups=None):
        return lax.all_to_all(
            jnp.broadcast_to(values[None], (count, *values.shape)), axis, 0, 0, axis_index_groups=groups
        )

    x_own = spread(x_src, "panel", units, same_core).reshape(-1, IN)
    prepared = prep(x_dst, weight, att_src, att_dst, grad_out, block_masks)
    x_other = lax.ppermute(x_own, "panel", siblings)
    place = lax.axis_index("panel").reshape(1)
    grad_dst, keep, send = local(
        x_own, x_other, x_dst, weight, att_src, att_dst, block_rows, block_cols, place, prepared
    )
    half = (keep + lax.ppermute(send, "panel", siblings).astype(F32)).astype(BF16)
    got = lax.all_to_all(half, "panel", 0, 0, axis_index_groups=same_core)
    unit = got.astype(F32).sum(axis=0).astype(BF16)
    total = spread(unit, "rep", lax.axis_size("rep")).astype(F32).sum(axis=0)
    grad_src = total[:BLK]
    small = spread(total[BLK:].astype(BF16), "panel", panels)
    grad_weight = small[:, :share].reshape(WIDTH // LANES, IN, LANES).transpose(1, 0, 2).reshape(IN, WIDTH)
    att = small[0, share:].astype(F32)
    return grad_src, grad_dst, grad_weight.astype(F32), att[:, :HEAD_DIM], att[:, HEAD_DIM:]


def solution(mesh):
    return jax.shard_map(
        shards,
        mesh=mesh,
        in_specs=(
            P("panel", None),
            P(("panel", "rep"), None),
            P(),
            P(),
            P(),
            P(("panel", "rep"), None),
            P(("panel", "rep")),
            P(("panel", "rep")),
            P(("panel", "rep"), None, None),
            P(("panel", "rep")),
        ),
        out_specs=(P("panel", None), P(("panel", "rep"), None), P(), P(), P()),
        check_vma=False,
    )
```

```python
import jax
import jax.numpy as jnp
from jax import lax
from jax.experimental import pallas as pl
from jax.experimental.pallas import tpu as pltpu
from jax.sharding import PartitionSpec as P

HEADS, HEAD_DIM, IN, WIDTH, BLK = 8, 64, 128, 512, 128
LOG2E = 1.4426950408889634
LANES = 128
F32, BF16 = jnp.float32, jnp.bfloat16
VMEM_BYTES = 40 << 20

NN = (((1,), (0,)), ((), ()))
NT = (((1,), (1,)), ((), ()))
TN = (((0,), (0,)), ((), ()))


def mm(a, b, dims=NN):
    return lax.dot_general(a, b, dims, preferred_element_type=F32)


def split2(values):
    hi = values.astype(BF16)
    return hi, (values - hi.astype(F32)).astype(BF16)


def split3(values):
    hi = values.astype(BF16)
    rest = values - hi.astype(F32)
    mid = rest.astype(BF16)
    return hi, mid, (rest - mid.astype(F32)).astype(BF16)


def head_rows(att):
    head = lax.broadcasted_iota(jnp.int32, (HEADS, WIDTH), 0)
    lane = lax.broadcasted_iota(jnp.int32, (HEADS, WIDTH), 1) // HEAD_DIM
    return jnp.where(head == lane, jnp.concatenate([att] * HEADS, axis=1), 0.0)


def feature_rows(att):
    flat = jnp.sum(head_rows(att), axis=0, keepdims=True)
    return jnp.broadcast_to(flat, (LANES, WIDTH)).T


def per_head(rows):
    width = rows.shape[1]
    return jnp.concatenate(
        [jnp.broadcast_to(rows[h : h + 1], (HEAD_DIM, width)) for h in range(HEADS)], axis=0
    )


def head_sums(values):
    return jnp.concatenate(
        [
            jnp.sum(values[h * HEAD_DIM : (h + 1) * HEAD_DIM], axis=0, keepdims=True)
            for h in range(HEADS)
        ],
        axis=0,
    )


def weight_and_slope(pre2):
    log = jnp.log2(1.0 + jnp.exp2(pre2))
    return jnp.exp2(0.2 * pre2 + 0.8 * log), 1.0 - 0.8 * jnp.exp2(-log)


def prepare(
    x_dst_hbm, weight_hbm, att_src_ref, att_dst_ref, grad_ref, mask_ref,
    proj_ref, grad_t_ref, mask_t_ref, score_ref, self_ref, slope_ref, pair_ref,
    x_dst_ref, weight_ref, x_sem, weight_sem,
):
    copies = (
        pltpu.make_async_copy(x_dst_hbm, x_dst_ref, x_sem),
        pltpu.make_async_copy(weight_hbm, weight_ref, weight_sem),
    )
    for copy in copies:
        copy.start()

    def turn(b, carry):
        mask_t_ref[b] = mask_ref[b].astype(F32).T
        return carry

    lax.fori_loop(0, mask_ref.shape[0], turn, 0, unroll=4)
    grad_t = grad_ref[...].astype(F32).T
    grad_t_ref[...] = grad_t.astype(BF16)
    parts = split3(head_rows(att_dst_ref[...])) + split3(head_rows(att_src_ref[...]))
    for copy in copies:
        copy.wait()
    weight_t = weight_ref[...].astype(F32).T.astype(BF16)
    proj = mm(weight_t, x_dst_ref[...], NT).astype(BF16)
    proj_ref[...] = proj
    scores = mm(jnp.concatenate(parts, axis=0), proj)
    score_d = (scores[0:8] + scores[8:16]) + scores[16:24]
    score_own = (scores[24:32] + scores[32:40]) + scores[40:48]
    for r in range(score_ref.shape[0]):
        score_ref[r] = score_d[:, r * BLK : (r + 1) * BLK] * LOG2E
    weight_self, slope_self = weight_and_slope((score_d + score_own) * LOG2E)
    self_ref[...] = weight_self
    slope_ref[...] = slope_self
    pair_ref[...] = head_sums(grad_t * proj.astype(F32))


def edges(
    rows_ref, cols_ref, place_ref,
    x_own_ref, x_other_ref, x_dst_hbm, weight_hbm, att_src_ref, att_dst_ref,
    proj_ref, grad_t_ref, mask_t_ref, score_ref, self_ref, slope_ref, pair_ref,
    grad_dst_ref, keep_ref, send_ref,
    proj_src, tiles, acc, scaled, scaled_c, own, grad_src_ref, grad_weight_ref, rows_out, score_cols, att_wide, x_all, x_dst_ref, weight_ref, x_sem, weight_sem,
):
    slots = mask_t_ref.shape[0]
    dest_blocks = acc.shape[0]
    ext = acc.shape[2]
    weight_copy = pltpu.make_async_copy(weight_hbm, weight_ref, weight_sem)
    x_dst_copy = pltpu.make_async_copy(x_dst_hbm, x_dst_ref, x_sem)
    weight_copy.start()
    x_dst_copy.start()
    acc[...] = jnp.zeros(acc.shape, F32)
    grad_src_ref[...] = jnp.zeros(grad_src_ref.shape, grad_src_ref.dtype)
    att_rows = jnp.concatenate(split3(head_rows(att_src_ref[...])), axis=0)
    weight_copy.wait()
    weight = weight_ref[...]
    weight_t = weight.astype(F32).T.astype(BF16)
    ones = jnp.ones((ext - HEAD_DIM, BLK), BF16)

    att_wide[...] = feature_rows(att_src_ref[...])

    core = place_ref[0] % 2
    half = x_own_ref.shape[0]
    x_all[0:half] = x_own_ref[...]
    x_all[half : 2 * half] = x_other_ref[...]

    def block(b):
        return pl.ds(pl.multiple_of(cols_ref[b] * BLK, BLK), BLK)

    def sources(b):
        col = cols_ref[b]
        place = (col % 2 + core) % 2 * half + col // 2 * BLK
        return x_all[pl.ds(pl.multiple_of(place, BLK), BLK), :]

    group = jnp.concatenate([sources(b) for b in range(slots)], axis=0)
    projs = mm(weight_t, group, NT).astype(BF16)
    scores = mm(att_rows, projs)
    score_t = (((scores[0:8] + scores[8:16]) + scores[16:24]) * LOG2E).T
    for b in range(slots):
        proj_src[b] = projs[:, b * BLK : (b + 1) * BLK]
        score_cols[b] = score_t[b * BLK : (b + 1) * BLK]

    def forward(b, carry):
        row = rows_ref[b]
        proj = proj_src[b]
        cols = score_cols[b]
        mask = mask_t_ref[b]
        score_d = score_ref[row]
        for h in range(HEADS):
            pre2 = jnp.broadcast_to(cols[:, h : h + 1], (BLK, BLK)) + score_d[h : h + 1]
            weight_e, slope = weight_and_slope(pre2)
            weight_e = weight_e * mask
            both = [weight_e.astype(BF16), (weight_e * slope).astype(BF16)]
            tiles[b, h, 0:BLK] = both[0]
            tiles[b, h, BLK : 2 * BLK] = both[1]
            pair = jnp.concatenate(both, axis=1)
            left = jnp.concatenate([proj[h * HEAD_DIM : (h + 1) * HEAD_DIM], ones], axis=0)
            acc[row, h] += mm(left, pair)
        return carry

    lax.fori_loop(0, slots, forward, 0, unroll=8)

    x_dst_copy.wait()
    self_att_rows, self_grad_rows, grad_d_rows = [], [], []
    for r in range(dest_blocks):
        lanes = slice(r * BLK, (r + 1) * BLK)
        self_w = self_ref[:, lanes]
        selfs, grads, dsts = [], [], []
        for h in range(HEADS):
            feats = slice(h * HEAD_DIM, (h + 1) * HEAD_DIM)
            sums = acc[r, h]
            w_self = self_w[h : h + 1]
            inv = 1.0 / (sums[HEAD_DIM : HEAD_DIM + 1, :BLK] + w_self)
            numer = sums[:HEAD_DIM, :BLK] + w_self * proj_ref[feats, lanes].astype(F32)
            grad = grad_t_ref[feats, lanes].astype(F32)
            part = (grad * inv).astype(BF16)
            part_wide = part.astype(F32)
            centred = jnp.sum(grad * numer, axis=0, keepdims=True) * inv
            centred_part = jnp.sum(part_wide * numer, axis=0, keepdims=True) * inv
            grad_d = (
                jnp.sum(part_wide * sums[:HEAD_DIM, BLK:], axis=0, keepdims=True)
                - centred_part * sums[HEAD_DIM : HEAD_DIM + 1, BLK:]
            )
            att_self = w_self * inv
            grad_self = (
                att_self * (pair_ref[h : h + 1, lanes] - centred) * slope_ref[h : h + 1, lanes]
            )
            scaled[r, h, 0:HEAD_DIM] = part
            c_hi, c_lo = split2(centred_part)
            scaled_c[r, h, 0:1] = c_hi.astype(F32)
            scaled_c[r, h, 1:2] = c_lo.astype(F32)
            selfs.append(att_self)
            grads.append(grad_self)
            dsts.append(grad_d + grad_self)
        self_att_rows.append(jnp.concatenate(selfs, axis=0))
        self_grad_rows.append(jnp.concatenate(grads, axis=0))
        grad_d_rows.append(jnp.concatenate(dsts, axis=0))
    for r in range(dest_blocks):
        for h in range(HEADS):
            scaled[r, h, HEAD_DIM:ext] = jnp.concatenate(
                [scaled_c[r, h, 0:2], jnp.zeros((ext - HEAD_DIM - 2, BLK), F32)], axis=0
            ).astype(BF16)

    att_src_wide = att_wide[...]
    att_dst_wide = feature_rows(att_dst_ref[...])
    grad_weight = jnp.zeros((WIDTH, IN), F32)
    att_sums = jnp.zeros((WIDTH, 32), F32)
    for r in range(dest_blocks):
        lanes = slice(r * BLK, (r + 1) * BLK)
        grad_proj = (
            per_head(self_att_rows[r]) * grad_t_ref[:, lanes].astype(F32)
            + per_head(self_grad_rows[r]) * att_src_wide
            + per_head(grad_d_rows[r]) * att_dst_wide
        ).astype(BF16)
        grad_dst_ref[lanes, :] = mm(weight, grad_proj).T
        grad_weight = grad_weight + mm(grad_proj, x_dst_ref[lanes, :])
        both = jnp.concatenate(split2(self_grad_rows[r]) + split2(grad_d_rows[r]), axis=0)
        att_sums = att_sums + mm(proj_ref[:, lanes], both, NT)
    grad_weight_ref[...] = grad_weight
    own[...] = att_sums

    def back(b):
        row = rows_ref[b]
        proj = proj_src[b]
        feats, grads = [], []
        for h in range(HEADS):
            out = mm(scaled[row, h], tiles[b, h], NT)
            feats.append(out[:HEAD_DIM, :BLK])
            proj_h = proj[h * HEAD_DIM : (h + 1) * HEAD_DIM].astype(F32)
            grads.append(
                jnp.sum(proj_h * out[:HEAD_DIM, BLK:], axis=0, keepdims=True)
                - (out[HEAD_DIM : HEAD_DIM + 1, BLK:] + out[HEAD_DIM + 1 : HEAD_DIM + 2, BLK:])
            )
        grad_s = jnp.concatenate(grads, axis=0)
        grad_proj = jnp.concatenate(feats, axis=0) + per_head(grad_s) * att_wide[...]
        return proj, grad_s, grad_proj.astype(BF16)

    def backward(step, carry):
        b = 2 * step
        projs, grads, parts = zip(back(b), back(b + 1))
        grad_proj = jnp.concatenate(parts, axis=1)
        into = mm(weight, grad_proj)
        x_pair = jnp.concatenate([sources(b), sources(b + 1)], axis=0)
        grad_weight_ref[...] += mm(grad_proj, x_pair)
        grad_s = jnp.concatenate(split2(jnp.concatenate(grads, axis=1)), axis=0)
        own[:, 0:16] += mm(jnp.concatenate(projs, axis=1), grad_s, NT)
        for k in range(2):
            grad_src_ref[block(b + k), :] += into[:, k * BLK : (k + 1) * BLK].T
        return carry

    lax.fori_loop(0, slots // 2, backward, 0, unroll=8)

    sums = own[...]
    head = lax.broadcasted_iota(jnp.int32, (WIDTH, HEADS), 1)
    feat = lax.broadcasted_iota(jnp.int32, (WIDTH, HEADS), 0) // HEAD_DIM
    pick = head == feat
    src = jnp.where(pick, sums[:, 0:8] + sums[:, 8:16], 0.0)
    dst = jnp.where(pick, sums[:, 16:24] + sums[:, 24:32], 0.0)
    low = lax.broadcasted_iota(jnp.int32, (HEADS, LANES), 1) < HEAD_DIM
    folded = []
    for part in (src, dst):
        part = part.T
        pair = sum(part[:, f : f + LANES] for f in range(0, WIDTH, LANES))
        folded.append(pair + pltpu.roll(pair, HEAD_DIM, axis=1))
    att8 = jnp.where(low, folded[0], folded[1])
    for f in range(0, WIDTH, LANES):
        rows_out[f : f + LANES, :] = grad_weight_ref[f : f + LANES, :].T

    units = send_ref.shape[0]
    share = WIDTH // (2 * units)

    def pack(u, carry):
        for other, out in ((0, keep_ref), (1, send_ref)):
            panel = 2 * u + (core + other) % 2
            start = pl.multiple_of(panel * BLK, BLK)
            w_start = pl.multiple_of(panel * share, share)
            unit = jnp.concatenate(
                [
                    grad_src_ref[pl.ds(start, BLK), :],
                    rows_out[pl.ds(w_start, share), :],
                    jnp.where(panel == 0, att8, 0.0),
                ],
                axis=0,
            )
            out[u] = unit.astype(out.dtype)
        return carry

    lax.fori_loop(0, units, pack, 0)


def prep(x_dst, weight, att_src, att_dst, grad_out, block_masks):
    slots = block_masks.shape[0]
    dest = x_dst.shape[0]
    dest_blocks = dest // BLK
    params = pltpu.CompilerParams(vmem_limit_bytes=VMEM_BYTES)
    rows8 = jax.ShapeDtypeStruct((HEADS, dest), F32)
    return pl.pallas_call(
        prepare,
        out_shape=[
            jax.ShapeDtypeStruct((WIDTH, dest), BF16),
            jax.ShapeDtypeStruct((WIDTH, dest), BF16),
            jax.ShapeDtypeStruct((slots, BLK, BLK), F32),
            jax.ShapeDtypeStruct((dest_blocks, HEADS, BLK), F32),
            rows8, rows8, rows8,
        ],
        in_specs=[pl.BlockSpec(memory_space=pltpu.HBM)] * 2 + [pl.BlockSpec(memory_space=pltpu.VMEM)] * 4,
        out_specs=[pl.BlockSpec(memory_space=pltpu.VMEM)] * 7,
        scratch_shapes=[
            pltpu.VMEM(x_dst.shape, BF16),
            pltpu.VMEM(weight.shape, BF16),
            pltpu.SemaphoreType.DMA,
            pltpu.SemaphoreType.DMA,
        ],
        compiler_params=params,
        cost_estimate=pl.CostEstimate(flops=2 * dest * IN * WIDTH, bytes_accessed=6 << 20, transcendentals=0),
        name="prepare",
    )(x_dst, weight, att_src, att_dst, grad_out, block_masks)


def local(x_own, x_other, x_dst, weight, att_src, att_dst, block_rows, block_cols, place, prepared):
    proj, grad_t, mask_t, score, self_w, slope, pair = prepared
    slots = mask_t.shape[0]
    dest = x_dst.shape[0]
    dest_blocks = dest // BLK
    sources = 2 * x_own.shape[0]
    panels = sources // BLK
    params = pltpu.CompilerParams(vmem_limit_bytes=VMEM_BYTES)
    ext = 72
    operands = (
        x_own, x_other, x_dst, weight, att_src, att_dst,
        proj, grad_t, mask_t, score, self_w, slope, pair,
    )
    units = panels // 2
    share = WIDTH // panels
    unit_rows = BLK + share + 8
    outs = [
        jax.ShapeDtypeStruct((dest, IN), F32),
        jax.ShapeDtypeStruct((units, unit_rows, LANES), F32),
        jax.ShapeDtypeStruct((units, unit_rows, LANES), BF16),
    ]
    return pl.pallas_call(
        edges,
        out_shape=outs,
        in_specs=[pl.BlockSpec(memory_space=pltpu.SMEM)] * 3
        + [
            pl.BlockSpec(memory_space=pltpu.HBM if o is x_dst or o is weight else pltpu.VMEM)
            for o in operands
        ],
        out_specs=[pl.BlockSpec(memory_space=pltpu.VMEM)] * len(outs),
        scratch_shapes=[
            pltpu.VMEM((slots, WIDTH, BLK), BF16),
            pltpu.VMEM((slots, HEADS, 2 * BLK, BLK), BF16),
            pltpu.VMEM((dest_blocks, HEADS, ext, 2 * BLK), F32),
            pltpu.VMEM((dest_blocks, HEADS, ext, BLK), BF16),
            pltpu.VMEM((dest_blocks, HEADS, 8, BLK), F32),
            pltpu.VMEM((WIDTH, 32), F32),
            pltpu.VMEM((sources, IN), F32),
            pltpu.VMEM((WIDTH, IN), F32),
            pltpu.VMEM((WIDTH, IN), F32),
            pltpu.VMEM((slots, BLK, HEADS), F32),
            pltpu.VMEM((WIDTH, LANES), F32),
            pltpu.VMEM((sources, IN), BF16),
            pltpu.VMEM(x_dst.shape, BF16),
            pltpu.VMEM(weight.shape, BF16),
            pltpu.SemaphoreType.DMA,
            pltpu.SemaphoreType.DMA,
        ],
        compiler_params=params,
        cost_estimate=pl.CostEstimate(flops=4 << 30, bytes_accessed=12 << 20, transcendentals=8 << 20),
        name="edges",
    )(block_rows, block_cols, place, *operands)


def shards(
    x_src, x_dst, weight, att_src, att_dst, grad_out, block_rows, block_cols, block_masks, block_counts
):
    panels = lax.axis_size("panel")
    units = panels // 2
    share = WIDTH // panels
    same_core = [[p for p in range(panels) if p % 2 == core] for core in range(2)]
    siblings = [(p, p ^ 1) for p in range(panels)]

    def spread(values, axis, count, groups=None):
        return lax.all_to_all(
            jnp.broadcast_to(values[None], (count, *values.shape)), axis, 0, 0, axis_index_groups=groups
        )

    x_own = spread(x_src, "panel", units, same_core).reshape(-1, IN)
    prepared = prep(x_dst, weight, att_src, att_dst, grad_out, block_masks)
    x_other = lax.ppermute(x_own, "panel", siblings)
    place = lax.axis_index("panel").reshape(1)
    grad_dst, keep, send = local(
        x_own, x_other, x_dst, weight, att_src, att_dst, block_rows, block_cols, place, prepared
    )
    half = (keep + lax.ppermute(send, "panel", siblings).astype(F32)).astype(BF16)
    got = lax.all_to_all(half, "panel", 0, 0, axis_index_groups=same_core)
    unit = got.astype(F32).sum(axis=0).astype(BF16)
    total = spread(unit, "rep", lax.axis_size("rep")).astype(F32).sum(axis=0)
    grad_src = total[:BLK]
    small = spread(total[BLK:].astype(BF16), "panel", panels)
    grad_weight = small[:, :share].reshape(WIDTH // LANES, IN, LANES).transpose(1, 0, 2).reshape(IN, WIDTH)
    att = small[0, share:].astype(F32)
    return grad_src, grad_dst, grad_weight.astype(F32), att[:, :HEAD_DIM], att[:, HEAD_DIM:]


def solution(mesh):
    return jax.shard_map(
        shards,
        mesh=mesh,
        in_specs=(
            P("panel", None),
            P(("panel", "rep"), None),
            P(),
            P(),
            P(),
            P(("panel", "rep"), None),
            P(("panel", "rep")),
            P(("panel", "rep")),
            P(("panel", "rep"), None, None),
            P(("panel", "rep")),
        ),
        out_specs=(P("panel", None), P(("panel", "rep"), None), P(), P(), P()),
        check_vma=False,
    )
```

```python
import jax
import jax.numpy as jnp
from jax import lax
from jax.experimental import pallas as pl
from jax.experimental.pallas import tpu as pltpu
from jax.sharding import PartitionSpec as P

HEADS, HEAD_DIM, IN, WIDTH, BLK = 8, 64, 128, 512, 128
LOG2E = 1.4426950408889634
LANES = 128
F32, BF16 = jnp.float32, jnp.bfloat16
VMEM_BYTES = 40 << 20

NN = (((1,), (0,)), ((), ()))
NT = (((1,), (1,)), ((), ()))
TN = (((0,), (0,)), ((), ()))


def mm(a, b, dims=NN):
    return lax.dot_general(a, b, dims, preferred_element_type=F32)


def split2(values):
    hi = values.astype(BF16)
    return hi, (values - hi.astype(F32)).astype(BF16)


def split3(values):
    hi = values.astype(BF16)
    rest = values - hi.astype(F32)
    mid = rest.astype(BF16)
    return hi, mid, (rest - mid.astype(F32)).astype(BF16)


def head_rows(att):
    head = lax.broadcasted_iota(jnp.int32, (HEADS, WIDTH), 0)
    lane = lax.broadcasted_iota(jnp.int32, (HEADS, WIDTH), 1) // HEAD_DIM
    return jnp.where(head == lane, jnp.concatenate([att] * HEADS, axis=1), 0.0)


def feature_rows(att):
    flat = jnp.sum(head_rows(att), axis=0, keepdims=True)
    return jnp.broadcast_to(flat, (LANES, WIDTH)).T


def per_head(rows):
    width = rows.shape[1]
    return jnp.concatenate(
        [jnp.broadcast_to(rows[h : h + 1], (HEAD_DIM, width)) for h in range(HEADS)], axis=0
    )


def head_sums(values):
    return jnp.concatenate(
        [
            jnp.sum(values[h * HEAD_DIM : (h + 1) * HEAD_DIM], axis=0, keepdims=True)
            for h in range(HEADS)
        ],
        axis=0,
    )


def weight_and_slope(pre2):
    log = jnp.log2(1.0 + jnp.exp2(pre2))
    return jnp.exp2(0.2 * pre2 + 0.8 * log), 1.0 - 0.8 * jnp.exp2(-log)


def prepare(
    x_dst_hbm, weight_hbm, att_src_ref, att_dst_ref, grad_ref, mask_ref,
    proj_ref, grad_t_ref, mask_t_ref, score_ref, self_ref, slope_ref, pair_ref,
    x_dst_ref, weight_ref, x_sem, weight_sem,
):
    copies = (
        pltpu.make_async_copy(x_dst_hbm, x_dst_ref, x_sem),
        pltpu.make_async_copy(weight_hbm, weight_ref, weight_sem),
    )
    for copy in copies:
        copy.start()

    def turn(b, carry):
        mask_t_ref[b] = mask_ref[b].astype(F32).T
        return carry

    lax.fori_loop(0, mask_ref.shape[0], turn, 0, unroll=4)
    grad_t = grad_ref[...].astype(F32).T
    grad_t_ref[...] = grad_t.astype(BF16)
    parts = split3(head_rows(att_dst_ref[...])) + split3(head_rows(att_src_ref[...]))
    for copy in copies:
        copy.wait()
    weight_t = weight_ref[...].astype(F32).T.astype(BF16)
    proj = mm(weight_t, x_dst_ref[...], NT).astype(BF16)
    proj_ref[...] = proj
    scores = mm(jnp.concatenate(parts, axis=0), proj)
    score_d = (scores[0:8] + scores[8:16]) + scores[16:24]
    score_own = (scores[24:32] + scores[32:40]) + scores[40:48]
    for r in range(score_ref.shape[0]):
        score_ref[r] = score_d[:, r * BLK : (r + 1) * BLK] * LOG2E
    weight_self, slope_self = weight_and_slope((score_d + score_own) * LOG2E)
    self_ref[...] = weight_self
    slope_ref[...] = slope_self
    pair_ref[...] = head_sums(grad_t * proj.astype(F32))


def edges(
    rows_ref, cols_ref, place_ref,
    x_own_ref, x_other_ref, x_dst_hbm, weight_hbm, att_src_ref, att_dst_ref,
    proj_ref, grad_t_ref, mask_t_ref, score_ref, self_ref, slope_ref, pair_ref,
    grad_dst_ref, keep_ref, send_ref,
    proj_src, tiles, acc, scaled, scaled_c, own, grad_src_ref, grad_weight_ref, rows_out, score_cols, att_wide, x_all, x_dst_ref, weight_ref, x_sem, weight_sem,
):
    slots = mask_t_ref.shape[0]
    dest_blocks = acc.shape[0]
    ext = acc.shape[2]
    weight_copy = pltpu.make_async_copy(weight_hbm, weight_ref, weight_sem)
    x_dst_copy = pltpu.make_async_copy(x_dst_hbm, x_dst_ref, x_sem)
    weight_copy.start()
    x_dst_copy.start()
    acc[...] = jnp.zeros(acc.shape, F32)
    grad_src_ref[...] = jnp.zeros(grad_src_ref.shape, grad_src_ref.dtype)
    att_rows = jnp.concatenate(split3(head_rows(att_src_ref[...])), axis=0)
    weight_copy.wait()
    weight = weight_ref[...]
    weight_t = weight.astype(F32).T.astype(BF16)
    ones = jnp.ones((ext - HEAD_DIM, BLK), BF16)

    att_wide[...] = feature_rows(att_src_ref[...])

    core = place_ref[0] % 2
    half = x_own_ref.shape[0]
    x_all[0:half] = x_own_ref[...]
    x_all[half : 2 * half] = x_other_ref[...]

    def block(b):
        return pl.ds(pl.multiple_of(cols_ref[b] * BLK, BLK), BLK)

    def sources(b):
        col = cols_ref[b]
        place = (col % 2 + core) % 2 * half + col // 2 * BLK
        return x_all[pl.ds(pl.multiple_of(place, BLK), BLK), :]

    group = jnp.concatenate([sources(b) for b in range(slots)], axis=0)
    projs = mm(weight_t, group, NT).astype(BF16)
    scores = mm(att_rows, projs)
    score_t = (((scores[0:8] + scores[8:16]) + scores[16:24]) * LOG2E).T
    for b in range(slots):
        proj_src[b] = projs[:, b * BLK : (b + 1) * BLK]
        score_cols[b] = score_t[b * BLK : (b + 1) * BLK]

    def forward(b, carry):
        row = rows_ref[b]
        proj = proj_src[b]
        cols = score_cols[b]
        mask = mask_t_ref[b]
        score_d = score_ref[row]
        for h in range(HEADS):
            pre2 = jnp.broadcast_to(cols[:, h : h + 1], (BLK, BLK)) + score_d[h : h + 1]
            weight_e, slope = weight_and_slope(pre2)
            weight_e = weight_e * mask
            both = [weight_e.astype(BF16), (weight_e * slope).astype(BF16)]
            tiles[b, h, 0:BLK] = both[0]
            tiles[b, h, BLK : 2 * BLK] = both[1]
            pair = jnp.concatenate(both, axis=1)
            left = jnp.concatenate([proj[h * HEAD_DIM : (h + 1) * HEAD_DIM], ones], axis=0)
            acc[row, h] += mm(left, pair)
        return carry

    lax.fori_loop(0, slots, forward, 0, unroll=8)

    x_dst_copy.wait()
    self_att_rows, self_grad_rows, grad_d_rows = [], [], []
    for r in range(dest_blocks):
        lanes = slice(r * BLK, (r + 1) * BLK)
        self_w = self_ref[:, lanes]
        selfs, grads, dsts = [], [], []
        for h in range(HEADS):
            feats = slice(h * HEAD_DIM, (h + 1) * HEAD_DIM)
            sums = acc[r, h]
            w_self = self_w[h : h + 1]
            denom = sums[HEAD_DIM : HEAD_DIM + 1, :BLK] + w_self
            inv = 1.0 / denom
            power = jnp.exp2(-jnp.round(jnp.log2(denom))).astype(BF16).astype(F32)
            near = 1.0 / (denom * power)
            numer = sums[:HEAD_DIM, :BLK] + w_self * proj_ref[feats, lanes].astype(F32)
            grad = grad_t_ref[feats, lanes].astype(F32)
            part = (grad * near).astype(BF16)
            part_wide = part.astype(F32)
            centred = jnp.sum(grad * numer, axis=0, keepdims=True) * inv
            centred_part = jnp.sum(part_wide * numer, axis=0, keepdims=True) * inv
            grad_d = (
                jnp.sum(part_wide * (sums[:HEAD_DIM, BLK:] * power), axis=0, keepdims=True)
                - centred_part * (sums[HEAD_DIM : HEAD_DIM + 1, BLK:] * power)
            )
            att_self = w_self * inv
            grad_self = (
                att_self * (pair_ref[h : h + 1, lanes] - centred) * slope_ref[h : h + 1, lanes]
            )
            scaled[r, h, 0:HEAD_DIM] = part
            c_hi, c_lo = split2(centred_part)
            scaled_c[r, h, 0:1] = c_hi.astype(F32)
            scaled_c[r, h, 1:2] = c_lo.astype(F32)
            scaled_c[r, h, 2:3] = power
            selfs.append(att_self)
            grads.append(grad_self)
            dsts.append(grad_d + grad_self)
        self_att_rows.append(jnp.concatenate(selfs, axis=0))
        self_grad_rows.append(jnp.concatenate(grads, axis=0))
        grad_d_rows.append(jnp.concatenate(dsts, axis=0))
    for r in range(dest_blocks):
        for h in range(HEADS):
            scaled[r, h, HEAD_DIM:ext] = jnp.concatenate(
                [scaled_c[r, h, 0:2], jnp.zeros((ext - HEAD_DIM - 2, BLK), F32)], axis=0
            ).astype(BF16)

    att_src_wide = att_wide[...]
    att_dst_wide = feature_rows(att_dst_ref[...])
    grad_weight = jnp.zeros((WIDTH, IN), F32)
    att_sums = jnp.zeros((WIDTH, 32), F32)
    for r in range(dest_blocks):
        lanes = slice(r * BLK, (r + 1) * BLK)
        grad_proj = (
            per_head(self_att_rows[r]) * grad_t_ref[:, lanes].astype(F32)
            + per_head(self_grad_rows[r]) * att_src_wide
            + per_head(grad_d_rows[r]) * att_dst_wide
        ).astype(BF16)
        grad_dst_ref[lanes, :] = mm(weight, grad_proj).T
        grad_weight = grad_weight + mm(grad_proj, x_dst_ref[lanes, :])
        both = jnp.concatenate(split2(self_grad_rows[r]) + split2(grad_d_rows[r]), axis=0)
        att_sums = att_sums + mm(proj_ref[:, lanes], both, NT)
    grad_weight_ref[...] = grad_weight
    own[...] = att_sums

    def back(b):
        row = rows_ref[b]
        proj = proj_src[b]
        feats, grads = [], []
        for h in range(HEADS):
            power = scaled_c[row, h, 2:3].astype(BF16)
            out = mm(scaled[row, h], tiles[b, h] * power, NT)
            feats.append(out[:HEAD_DIM, :BLK])
            proj_h = proj[h * HEAD_DIM : (h + 1) * HEAD_DIM].astype(F32)
            grads.append(
                jnp.sum(proj_h * out[:HEAD_DIM, BLK:], axis=0, keepdims=True)
                - (out[HEAD_DIM : HEAD_DIM + 1, BLK:] + out[HEAD_DIM + 1 : HEAD_DIM + 2, BLK:])
            )
        grad_s = jnp.concatenate(grads, axis=0)
        grad_proj = jnp.concatenate(feats, axis=0) + per_head(grad_s) * att_wide[...]
        return proj, grad_s, grad_proj.astype(BF16)

    def backward(step, carry):
        b = 2 * step
        projs, grads, parts = zip(back(b), back(b + 1))
        grad_proj = jnp.concatenate(parts, axis=1)
        into = mm(weight, grad_proj)
        x_pair = jnp.concatenate([sources(b), sources(b + 1)], axis=0)
        grad_weight_ref[...] += mm(grad_proj, x_pair)
        grad_s = jnp.concatenate(split2(jnp.concatenate(grads, axis=1)), axis=0)
        own[:, 0:16] += mm(jnp.concatenate(projs, axis=1), grad_s, NT)
        for k in range(2):
            grad_src_ref[block(b + k), :] += into[:, k * BLK : (k + 1) * BLK].T
        return carry

    lax.fori_loop(0, slots // 2, backward, 0, unroll=8)

    sums = own[...]
    head = lax.broadcasted_iota(jnp.int32, (WIDTH, HEADS), 1)
    feat = lax.broadcasted_iota(jnp.int32, (WIDTH, HEADS), 0) // HEAD_DIM
    pick = head == feat
    src = jnp.where(pick, sums[:, 0:8] + sums[:, 8:16], 0.0)
    dst = jnp.where(pick, sums[:, 16:24] + sums[:, 24:32], 0.0)
    low = lax.broadcasted_iota(jnp.int32, (HEADS, LANES), 1) < HEAD_DIM
    folded = []
    for part in (src, dst):
        part = part.T
        pair = sum(part[:, f : f + LANES] for f in range(0, WIDTH, LANES))
        folded.append(pair + pltpu.roll(pair, HEAD_DIM, axis=1))
    att8 = jnp.where(low, folded[0], folded[1])
    for f in range(0, WIDTH, LANES):
        rows_out[f : f + LANES, :] = grad_weight_ref[f : f + LANES, :].T

    units = send_ref.shape[0]
    share = WIDTH // (2 * units)

    def pack(u, carry):
        for other, out in ((0, keep_ref), (1, send_ref)):
            panel = 2 * u + (core + other) % 2
            start = pl.multiple_of(panel * BLK, BLK)
            w_start = pl.multiple_of(panel * share, share)
            unit = jnp.concatenate(
                [
                    grad_src_ref[pl.ds(start, BLK), :],
                    rows_out[pl.ds(w_start, share), :],
                    jnp.where(panel == 0, att8, 0.0),
                ],
                axis=0,
            )
            out[u] = unit.astype(out.dtype)
        return carry

    lax.fori_loop(0, units, pack, 0)


def prep(x_dst, weight, att_src, att_dst, grad_out, block_masks):
    slots = block_masks.shape[0]
    dest = x_dst.shape[0]
    dest_blocks = dest // BLK
    params = pltpu.CompilerParams(vmem_limit_bytes=VMEM_BYTES)
    rows8 = jax.ShapeDtypeStruct((HEADS, dest), F32)
    return pl.pallas_call(
        prepare,
        out_shape=[
            jax.ShapeDtypeStruct((WIDTH, dest), BF16),
            jax.ShapeDtypeStruct((WIDTH, dest), BF16),
            jax.ShapeDtypeStruct((slots, BLK, BLK), F32),
            jax.ShapeDtypeStruct((dest_blocks, HEADS, BLK), F32),
            rows8, rows8, rows8,
        ],
        in_specs=[pl.BlockSpec(memory_space=pltpu.HBM)] * 2 + [pl.BlockSpec(memory_space=pltpu.VMEM)] * 4,
        out_specs=[pl.BlockSpec(memory_space=pltpu.VMEM)] * 7,
        scratch_shapes=[
            pltpu.VMEM(x_dst.shape, BF16),
            pltpu.VMEM(weight.shape, BF16),
            pltpu.SemaphoreType.DMA,
            pltpu.SemaphoreType.DMA,
        ],
        compiler_params=params,
        cost_estimate=pl.CostEstimate(flops=2 * dest * IN * WIDTH, bytes_accessed=6 << 20, transcendentals=0),
        name="prepare",
    )(x_dst, weight, att_src, att_dst, grad_out, block_masks)


def local(x_own, x_other, x_dst, weight, att_src, att_dst, block_rows, block_cols, place, prepared):
    proj, grad_t, mask_t, score, self_w, slope, pair = prepared
    slots = mask_t.shape[0]
    dest = x_dst.shape[0]
    dest_blocks = dest // BLK
    sources = 2 * x_own.shape[0]
    panels = sources // BLK
    params = pltpu.CompilerParams(vmem_limit_bytes=VMEM_BYTES)
    ext = 72
    operands = (
        x_own, x_other, x_dst, weight, att_src, att_dst,
        proj, grad_t, mask_t, score, self_w, slope, pair,
    )
    units = panels // 2
    share = WIDTH // panels
    unit_rows = BLK + share + 8
    outs = [
        jax.ShapeDtypeStruct((dest, IN), F32),
        jax.ShapeDtypeStruct((units, unit_rows, LANES), F32),
        jax.ShapeDtypeStruct((units, unit_rows, LANES), BF16),
    ]
    return pl.pallas_call(
        edges,
        out_shape=outs,
        in_specs=[pl.BlockSpec(memory_space=pltpu.SMEM)] * 3
        + [
            pl.BlockSpec(memory_space=pltpu.HBM if o is x_dst or o is weight else pltpu.VMEM)
            for o in operands
        ],
        out_specs=[pl.BlockSpec(memory_space=pltpu.VMEM)] * len(outs),
        scratch_shapes=[
            pltpu.VMEM((slots, WIDTH, BLK), BF16),
            pltpu.VMEM((slots, HEADS, 2 * BLK, BLK), BF16),
            pltpu.VMEM((dest_blocks, HEADS, ext, 2 * BLK), F32),
            pltpu.VMEM((dest_blocks, HEADS, ext, BLK), BF16),
            pltpu.VMEM((dest_blocks, HEADS, 8, BLK), F32),
            pltpu.VMEM((WIDTH, 32), F32),
            pltpu.VMEM((sources, IN), F32),
            pltpu.VMEM((WIDTH, IN), F32),
            pltpu.VMEM((WIDTH, IN), F32),
            pltpu.VMEM((slots, BLK, HEADS), F32),
            pltpu.VMEM((WIDTH, LANES), F32),
            pltpu.VMEM((sources, IN), BF16),
            pltpu.VMEM(x_dst.shape, BF16),
            pltpu.VMEM(weight.shape, BF16),
            pltpu.SemaphoreType.DMA,
            pltpu.SemaphoreType.DMA,
        ],
        compiler_params=params,
        cost_estimate=pl.CostEstimate(flops=4 << 30, bytes_accessed=12 << 20, transcendentals=8 << 20),
        name="edges",
    )(block_rows, block_cols, place, *operands)


def shards(
    x_src, x_dst, weight, att_src, att_dst, grad_out, block_rows, block_cols, block_masks, block_counts
):
    panels = lax.axis_size("panel")
    units = panels // 2
    share = WIDTH // panels
    same_core = [[p for p in range(panels) if p % 2 == core] for core in range(2)]
    siblings = [(p, p ^ 1) for p in range(panels)]

    def spread(values, axis, count, groups=None):
        return lax.all_to_all(
            jnp.broadcast_to(values[None], (count, *values.shape)), axis, 0, 0, axis_index_groups=groups
        )

    x_own = spread(x_src, "panel", units, same_core).reshape(-1, IN)
    prepared = prep(x_dst, weight, att_src, att_dst, grad_out, block_masks)
    x_other = lax.ppermute(x_own, "panel", siblings)
    place = lax.axis_index("panel").reshape(1)
    grad_dst, keep, send = local(
        x_own, x_other, x_dst, weight, att_src, att_dst, block_rows, block_cols, place, prepared
    )
    half = (keep + lax.ppermute(send, "panel", siblings).astype(F32)).astype(BF16)
    got = lax.all_to_all(half, "panel", 0, 0, axis_index_groups=same_core)
    unit = got.astype(F32).sum(axis=0).astype(BF16)
    total = spread(unit, "rep", lax.axis_size("rep")).astype(F32).sum(axis=0)
    grad_src = total[:BLK]
    small = spread(total[BLK:].astype(BF16), "panel", panels)
    grad_weight = small[:, :share].reshape(WIDTH // LANES, IN, LANES).transpose(1, 0, 2).reshape(IN, WIDTH)
    att = small[0, share:].astype(F32)
    return grad_src, grad_dst, grad_weight.astype(F32), att[:, :HEAD_DIM], att[:, HEAD_DIM:]


def solution(mesh):
    return jax.shard_map(
        shards,
        mesh=mesh,
        in_specs=(
            P("panel", None),
            P(("panel", "rep"), None),
            P(),
            P(),
            P(),
            P(("panel", "rep"), None),
            P(("panel", "rep")),
            P(("panel", "rep")),
            P(("panel", "rep"), None, None),
            P(("panel", "rep")),
        ),
        out_specs=(P("panel", None), P(("panel", "rep"), None), P(), P(), P()),
        check_vma=False,
    )
```
